512 devices in a mesh: cp: 8 (over y_hi, x), dp: 64 (over y_lo, z, core).
Axes of the slice: x: 4, y: 8 (y_hi: 2, y_lo: 4; y = y_hi * 4 + y_lo), z: 8, core: 2. Of those that a mesh axis runs over, the one named last changes fastest.
Arguments:
- queries: bfloat16 [64, 1536, 512], P('dp', 'cp'), may hold values from -6 to 6
- key_rows: bfloat16 [64, 1536, 512], P('dp', 'cp'), may hold values from -6 to 6
- value_rows: bfloat16 [64, 1536, 512], P('dp', 'cp'), may hold values from -6 to 6
- stream_in: bfloat16 [64, 1536, 1024], P('dp', 'cp'), may hold values from -6 to 6
- out_grad: bfloat16 [64, 1536, 1024], P('dp', 'cp'), may hold values from -6 to 6
- out_weight: bfloat16 [512, 1024], P('cp'), may hold values from -0.25 to 0.25
- conv_weight: float32 [7, 1024], replicated, may hold values from -3 to 3
- lengths: int32 [64], P('dp'), may hold values from 768 to 1536, as said below
- offsets: int32 [64, 2], P('dp'), may hold values from 0 to 2, as said below
Outputs:
- query_grad: bfloat16 [64, 1536, 512], P('dp', 'cp')
- key_grad: bfloat16 [64, 1536, 512], P('dp', 'cp')
- value_grad: bfloat16 [64, 1536, 512], P('dp', 'cp')
- stream_grad: bfloat16 [64, 1536, 1024], P('dp', 'cp')
- weight_grad: float32 [512, 1024], P('cp')
- conv_grad: float32 [7, 1024], replicated
The draws below stay inside these ranges and needn't reach their ends.
Inputs may be any that keep to these rules, and one draw needn't show every extreme that they name: `lengths`: each a multiple of 24; some utterance has exactly 1536 frames. `offsets`: column 0 is the number of earlier blocks that a block attends, at most 2; column 1 the number of later blocks, at most 1; some utterance has 2 and 1.
All inputs are finite; a program needn't handle non-finite values.
Results may differ from the reference program's by a relative error of at most 0.0069.
Values may be sent and summed in bfloat16 or wider, within the bound.
A program may use at most 64 MiB of HBM per device.

```python
import jax
import jax.numpy as jnp
from jax import lax

D = 1024
HEADS = 8
HSZ = 64
BLK = 24
KW = 7
HD = 512
T_SIZE = 1536
UTTS = 64


def base_field(key, salt):
    return jnp.clip(jax.random.normal(jax.random.fold_in(key, salt), (UTTS, T_SIZE, HD), jnp.float32), -5.0, 5.0)


def draw_queries(key, part):
    field = base_field(key, 11)
    return field.astype(jnp.bfloat16)


def draw_key_rows(key, part):
    field = base_field(key, 21)
    return field.astype(jnp.bfloat16)


def draw_lengths(key, part):
    block_count = T_SIZE // BLK
    counts = jax.random.randint(jax.random.fold_in(key, 3), (UTTS,), block_count // 2, block_count + 1)
    full_at = jax.random.randint(jax.random.fold_in(key, 4), (), 0, UTTS)
    counts = jnp.where(jnp.arange(UTTS) == full_at, block_count, counts)
    return (counts * BLK).astype(jnp.int32)


def draw_offsets(key, part):
    before = jax.random.randint(jax.random.fold_in(key, 5), (UTTS,), 0, 3)
    after = jax.random.randint(jax.random.fold_in(key, 6), (UTTS,), 0, 2)
    widest = jax.random.randint(jax.random.fold_in(key, 9), (), 0, UTTS)
    chosen = jnp.arange(UTTS) == widest
    before = jnp.where(chosen, 2, before)
    after = jnp.where(chosen, 1, after)
    return jnp.stack([before, after], 1).astype(jnp.int32)


def level_of(key, shape, shards, low, top_value):
    loudness = 1.0
    for position, shards_of in shards:
        steps = jax.random.uniform(jax.random.fold_in(jax.random.fold_in(key, 6), position), (shards_of,), jnp.float32, low / len(shards), top_value / len(shards))
        loudness = loudness * jnp.repeat(jnp.exp(steps), shape[position] // shards_of).reshape((-1,) + (1,) * (len(shape) - 1 - position))
    return loudness


def bell_draw(key, shape, deviation, limit, cuts=(), kind=jnp.bfloat16):
    values = deviation * jax.random.normal(key, shape, jnp.float32)
    if cuts:
        values = values * level_of(key, shape, cuts, -0.22, 0.18)
    return jnp.clip(values, -limit, limit).astype(kind)


def setup_inputs(seed: int = 0) -> dict:
    arg_keys = jax.random.split(jax.random.key(seed), 10)
    queries = draw_queries(jax.random.fold_in(arg_keys[9], 71), 0)
    key_rows = draw_key_rows(jax.random.fold_in(arg_keys[9], 71), 0)
    value_rows = bell_draw(arg_keys[2], (UTTS, T_SIZE, HD), 1.0, 6.0, ((0, 64), (1, 8)))
    stream_in = bell_draw(arg_keys[3], (UTTS, T_SIZE, D), 1.0, 6.0, ((0, 64), (1, 8)))
    out_grad = bell_draw(arg_keys[4], (UTTS, T_SIZE, D), 1.0, 6.0, ((0, 64), (1, 8)))
    out_weight = bell_draw(arg_keys[5], (HD, D), HD ** -0.5, 0.25, ((0, 8),))
    conv_weight = bell_draw(arg_keys[6], (KW, D), 0.4, 3.0, (), jnp.float32)
    lengths = draw_lengths(jax.random.fold_in(arg_keys[9], 71), 0)
    offsets = draw_offsets(jax.random.fold_in(arg_keys[9], 71), 0)
    return dict(queries=queries, key_rows=key_rows, value_rows=value_rows, stream_in=stream_in, out_grad=out_grad, out_weight=out_weight, conv_weight=conv_weight, lengths=lengths, offsets=offsets)


neg_big = -1e30


def rounded(values):
    return lax.optimization_barrier(values.astype(jnp.bfloat16)).astype(jnp.float32)


def one_utterance(query_rows, key_local, value_local, stream_rows, grad_rows, length, offset_pair, out_weight, conv_weight):
    score_scale = HSZ ** -0.5
    block_count = T_SIZE // BLK
    window_len = 4 * BLK
    half_width = KW // 2
    frames = jnp.arange(T_SIZE, dtype=jnp.int32)
    valid_rows = (frames < length).astype(jnp.float32)

    def windows_of(array):
        padded = jnp.pad(array, ((2 * BLK, BLK), (0, 0)))
        slabs = [padded[shift_at * BLK: shift_at * BLK + T_SIZE].reshape(block_count, BLK, -1) for shift_at in range(4)]
        return jnp.stack(slabs, 1).reshape(block_count, window_len, HEADS, HSZ)

    key_win = windows_of(key_local).astype(jnp.float32)
    value_win = windows_of(value_local).astype(jnp.float32)
    query_blk = query_rows.astype(jnp.float32).reshape(block_count, BLK, HEADS, HSZ)
    within = jnp.arange(window_len, dtype=jnp.int32)
    key_frames = jnp.arange(block_count, dtype=jnp.int32)[:, None] * BLK + within[None, :] - 2 * BLK
    relative = within // BLK - 2
    in_reach = (relative >= -offset_pair[0]) & (relative <= offset_pair[1])
    allowed = in_reach[None, :] & (key_frames >= 0) & (key_frames < length)
    scores = jnp.einsum('nqhd,nkhd->nhqk', query_blk, key_win) * score_scale
    masked = jnp.where(allowed[:, None, None, :], scores, neg_big)
    top_score = jnp.max(masked, axis=3, keepdims=True)
    exp_terms = jnp.exp(masked - top_score)
    softmax_w = exp_terms / jnp.sum(exp_terms, axis=3, keepdims=True)
    weight_b = rounded(softmax_w)
    attended = jnp.einsum('nhqk,nkhd->nqhd', weight_b, value_win).reshape(T_SIZE, HD)
    attended = (attended * valid_rows[:, None]).astype(jnp.bfloat16)
    projected = jnp.dot(attended, out_weight, preferred_element_type=jnp.float32)
    mixed_rows = (stream_rows.astype(jnp.float32) + projected) * valid_rows[:, None]
    grad_masked = grad_rows * valid_rows[:, None].astype(grad_rows.dtype)
    grad_pad = jnp.pad(grad_masked.astype(jnp.float32), ((half_width, half_width), (0, 0)))
    conv_sum = jnp.zeros((T_SIZE, D), jnp.float32)
    conv_terms = []
    for tap in range(KW):
        shifted = grad_pad[2 * half_width - tap: 2 * half_width - tap + T_SIZE]
        conv_sum = conv_sum + conv_weight[tap][None, :] * shifted
        conv_terms.append(jnp.sum(mixed_rows * shifted, axis=0))
    conv_local = jnp.stack(conv_terms, 0)
    stream_grad = (conv_sum * valid_rows[:, None]).astype(jnp.bfloat16)
    weight_term = jnp.dot(attended.T, stream_grad, preferred_element_type=jnp.float32)
    attn_grad = jnp.dot(stream_grad, out_weight.T, preferred_element_type=jnp.float32).astype(jnp.bfloat16)
    grad_blk = attn_grad.astype(jnp.float32).reshape(block_count, BLK, HEADS, HSZ)
    dprob = jnp.einsum('nqhd,nkhd->nhqk', grad_blk, value_win)
    inner = jnp.sum(softmax_w * dprob, axis=3, keepdims=True)
    dscore = rounded(softmax_w * (dprob - inner))
    query_grad = (jnp.einsum('nhqk,nkhd->nqhd', dscore, key_win) * score_scale).reshape(T_SIZE, HD).astype(jnp.bfloat16)
    key_win_grad = jnp.einsum('nhqk,nqhd->nkhd', dscore, query_blk) * score_scale
    value_win_grad = jnp.einsum('nhqk,nqhd->nkhd', weight_b, grad_blk)

    def fold_back(window_grad):
        parts = window_grad.reshape(block_count, 4, BLK, HD)
        total = jnp.zeros((block_count + 3, BLK, HD), jnp.float32)
        for shift_at in range(4):
            total = total + jnp.pad(parts[:, shift_at], ((shift_at, 3 - shift_at), (0, 0), (0, 0)))
        return total[2:block_count + 2].reshape(T_SIZE, HD).astype(jnp.bfloat16)

    return query_grad, fold_back(key_win_grad), fold_back(value_win_grad), stream_grad, weight_term, conv_local


def reference(queries, key_rows, value_rows, stream_in, out_grad, out_weight, conv_weight, lengths, offsets):
    def scan_step(running, per_utt):
        results = one_utterance(*per_utt, out_weight, conv_weight)
        return (running[0] + results[4], running[1] + results[5]), results[:4]

    start_acc = (jnp.zeros((HD, D), jnp.float32), jnp.zeros((KW, D), jnp.float32))
    sums, grads = lax.scan(scan_step, start_acc, (queries, key_rows, value_rows, stream_in, out_grad, lengths, offsets))
    return grads[0], grads[1], grads[2], grads[3], sums[0], sums[1]
```

```python
import jax
import jax.numpy as jnp
from jax import lax
from jax.experimental import pallas as pl
from jax.experimental.pallas import tpu as pltpu
from jax.sharding import PartitionSpec as P

HSZ = 64
BLK = 24
KW = 7
ROWS = 192
HD = 512
D = 1024
HALF = 512
NX, NY, NYL, NZ = 4, 8, 4, 8
NC = 2
CW = HALF // NC
QT = 48
KT = 128
EXT = 272
GEXT = 224
NEG = -1e30
SCALE = HSZ ** -0.5
BF = jnp.bfloat16
F32 = jnp.float32
MESH = pl.DeviceIdType.MESH

CONTRACT_LAST = (((1,), (1,)), ((), ()))
CONTRACT_FIRST = (((0,), (0,)), ((), ()))
PLAIN = (((1,), (0,)), ((), ()))


def dot(a, b, dims):
    return lax.dot_general(a, b, dims, preferred_element_type=F32)


def kernel(
    len_ref, off_ref, q_in, k_in, v_in, s_in, g_in, w_in, cw_ref,
    qg_out, kg_out, vg_out, sg_out, wg_out, cg_out,
    kext, vext, qbuf, sbuf, gext, gf, wh, a_own, a_par, sg, s2p, ag, psave,
    kgacc, vgacc, to_prev, to_next, from_next, from_prev,
    qg_v, kg_v, vg_v, wg_v, cg_v,
    xs, xr, ys, yr, zr, fin,
    cpart, cpr, csx, cxr, cy, cz, cx,
    loc, out_sem, hs, hr, ws, wr, ps, pr, xss, xrs, yss, yrs, zss, zrs, fss, frs, css, crs,
):
    cp = lax.axis_index("cp")
    dp = lax.axis_index("dp")
    yh = cp // NX
    x = cp % NX
    core = dp % 2
    z = (dp // 2) % NZ
    yl = dp // (2 * NZ)
    y = yh * NYL + yl

    def dev(y_to, x_to, z_to, core_to):
        return {
            "cp": (y_to // NYL) * NX + x_to,
            "dp": ((y_to % NYL) * NZ + z_to) * 2 + core_to,
        }

    def x_peer(k):
        return dev(y, (x + k) % NX, z, core)

    def y_peer(k):
        return dev((y + k) % NY, x, z, core)

    def z_peer(k):
        return dev(y, x, (z + k) % NZ, core)

    def yl_peer(k):
        return dev(yh * NYL + (yl + k) % NYL, x, z, core)

    partner = dev(y, x, z, 1 - core)
    nxt = {"cp": (cp + 1) % 8, "dp": dp}
    prv = {"cp": (cp + 7) % 8, "dp": dp}
    across = {"cp": (cp + 4) % 8, "dp": dp}

    def rc(src, dst, ssem, rsem, to):
        return pltpu.make_async_remote_copy(
            src_ref=src, dst_ref=dst, send_sem=ssem, recv_sem=rsem,
            device_id=to, device_id_type=MESH,
        )

    sent = []

    def send(src, dst, ssem, rsem, to):
        c = rc(src, dst, ssem, rsem, to)
        c.start()
        sent.append(c)

    def arrived(dst, rsem, ssem, to):
        rc(dst, dst, ssem, rsem, to).wait_recv()

    barrier = pltpu.get_barrier_semaphore()
    greet = [y_peer(k) for k in (4, 3, 5, 2, 6, 1, 7)]
    greet += [z_peer(k) for k in (4, 3, 5, 2, 6, 1, 7)]
    greet += [nxt, prv] + [x_peer(k) for k in (2, 1, 3)] + [partner]
    for to in greet:
        pl.semaphore_signal(barrier, inc=1, device_id=to, device_id_type=MESH)

    c512 = pl.multiple_of(core * HALF, HALF)
    cprow = pl.multiple_of(cp * 64, 64)
    orow = pl.multiple_of(((cp + 4) % 8) * 64, 64)
    ylrow = pl.multiple_of(yl * 16, 16)
    wq_mine = pl.multiple_of(cp * 64 + yl * 16, 16)
    wq_other = pl.multiple_of(((cp + 4) % 8) * 64 + yl * 16, 16)

    loads = [
        pltpu.make_async_copy(k_in.at[0], kext.at[pl.ds(48, ROWS)], loc.at[0]),
        pltpu.make_async_copy(q_in.at[0], qbuf, loc.at[1]),
        pltpu.make_async_copy(v_in.at[0], vext.at[pl.ds(48, ROWS)], loc.at[2]),
        pltpu.make_async_copy(g_in.at[0], gext.at[pl.ds(16, ROWS)], loc.at[3]),
        pltpu.make_async_copy(w_in.at[:, pl.ds(0, HALF)], wh.at[0, pl.ds(cprow, 64)], loc.at[4]),
        pltpu.make_async_copy(w_in.at[:, pl.ds(HALF, HALF)], wh.at[1, pl.ds(cprow, 64)], loc.at[5]),
        pltpu.make_async_copy(s_in.at[0], sbuf, loc.at[6]),
    ]
    for c in loads:
        c.start()

    pl.semaphore_wait(barrier, len(greet))

    gi, ki, vi = g_in.at[0], k_in.at[0], v_in.at[0]
    send(gi.at[pl.ds(176, 16)], gext.at[pl.ds(0, 16)], hs.at[0], hr.at[0], nxt)
    send(gi.at[pl.ds(0, 16)], gext.at[pl.ds(208, 16)], hs.at[1], hr.at[1], prv)
    send(ki.at[pl.ds(144, 48)], kext.at[pl.ds(0, 48)], hs.at[2], hr.at[2], nxt)
    send(ki.at[pl.ds(0, 32)], kext.at[pl.ds(240, 32)], hs.at[3], hr.at[3], prv)
    send(vi.at[pl.ds(144, 48)], vext.at[pl.ds(0, 48)], hs.at[4], hr.at[4], nxt)
    send(vi.at[pl.ds(0, 32)], vext.at[pl.ds(240, 32)], hs.at[5], hr.at[5], prv)
    send(
        w_in.at[pl.ds(ylrow, 16), pl.ds(c512, HALF)],
        wh.at[core, pl.ds(wq_mine, 16)], ws.at[0], wr.at[0], across,
    )
    for k in range(1, NX):
        send(
            w_in.at[:, pl.ds(c512, HALF)],
            wh.at[core, pl.ds(cprow, 64)], ws.at[k], wr.at[k], x_peer(k),
        )

    length = len_ref[0]
    back = off_ref[0, 0]
    ahead = off_ref[0, 1]
    lane = lax.broadcasted_iota(jnp.int32, (1, 256), 1)
    head_f = [((lane // HSZ) == h).astype(F32) for h in range(4)]
    head_b = [m.astype(BF) for m in head_f]
    row_i = lax.broadcasted_iota(jnp.int32, (4 * QT, KT), 0)
    col_i = lax.broadcasted_iota(jnp.int32, (4 * QT, KT), 1)
    rel = col_i // BLK - 2 - (row_i % QT) // BLK
    reach = (rel >= -back) & (rel <= ahead)

    def stacked(block):
        return jnp.concatenate([block * head_b[h] for h in range(4)], axis=0)

    def unstacked(block):
        total = block[0:QT] * head_f[0]
        for h in range(1, 4):
            total = total + block[h * QT:(h + 1) * QT] * head_f[h]
        return total

    def forward_tile(i):
        r0 = pl.multiple_of(i * QT, 16)
        key_frame = cp * ROWS + i * QT - 2 * BLK + col_i
        ok = reach & (key_frame >= 0) & (key_frame < length)
        frame = cp * ROWS + i * QT + lax.broadcasted_iota(jnp.int32, (QT, 1), 0)
        valid = (frame < length).astype(F32)
        for g in range(2):
            cols = slice(256 * g, 256 * g + 256)
            kk = kext[pl.ds(r0, KT), cols]
            vv = vext[pl.ds(r0, KT), cols]
            qs = stacked(qbuf[pl.ds(r0, QT), cols])
            s = jnp.where(ok, dot(qs, kk, CONTRACT_LAST) * SCALE, NEG)
            e = jnp.exp(s - jnp.max(s, axis=1, keepdims=True))
            p = e / jnp.sum(e, axis=1, keepdims=True)
            psave[i, g] = p
            o = unstacked(dot(p.astype(BF), vv, PLAIN))
            a_own[pl.ds(r0, QT), cols] = (o * valid).astype(BF)

    for n in (0, 1, 2):
        loads[n].wait()

    def inner_fwd(t, carry):
        forward_tile(1 + t)
        return carry

    lax.fori_loop(0, 2, inner_fwd, 0)

    loads[3].wait()
    arrived(gext.at[pl.ds(0, 16)], hr.at[0], hs.at[0], nxt)
    arrived(gext.at[pl.ds(208, 16)], hr.at[1], hs.at[1], nxt)
    g_frame = cp * ROWS - 16 + lax.broadcasted_iota(jnp.int32, (GEXT, KT), 0)
    g_ok = (g_frame >= 0) & (g_frame < length)
    t_frame = cp * ROWS + lax.broadcasted_iota(jnp.int32, (ROWS, KT), 0)
    t_valid = (t_frame < length).astype(F32)

    def conv_chunk(n, carry):
        lanes = pl.ds(pl.multiple_of(n * 128, 128), 128)
        gf[n] = jnp.where(g_ok, gext[:, lanes].astype(F32), 0.0)
        acc = jnp.zeros((ROWS, 128), F32)
        for j in range(KW):
            acc = acc + cw_ref[pl.ds(j, 1), lanes] * gf[n, pl.ds(19 - j, ROWS), :]
        at = pl.ds(pl.multiple_of((n % 4) * 128, 128), 128)
        sg[n // 4, :, at] = (acc * t_valid).astype(BF)
        return carry

    lax.fori_loop(0, 8, conv_chunk, 0)
    send(sg.at[1 - core], s2p, ps.at[0], pr.at[0], partner)
    outs = [
        pltpu.make_async_copy(sg.at[0], sg_out.at[0, :, pl.ds(0, HALF)], out_sem.at[0]),
        pltpu.make_async_copy(sg.at[1], sg_out.at[0, :, pl.ds(HALF, HALF)], out_sem.at[1]),
    ]
    outs[0].start()
    outs[1].start()

    quarter = wh.at[core, pl.ds(wq_other, 16)]
    arrived(quarter, wr.at[0], ws.at[0], across)
    for k in range(1, NYL):
        send(quarter, quarter, ws.at[3 + k], wr.at[3 + k], yl_peer(k))

    arrived(kext.at[pl.ds(0, 48)], hr.at[2], hs.at[2], nxt)
    arrived(kext.at[pl.ds(240, 32)], hr.at[3], hs.at[3], nxt)
    arrived(vext.at[pl.ds(0, 48)], hr.at[4], hs.at[4], nxt)
    arrived(vext.at[pl.ds(240, 32)], hr.at[5], hs.at[5], nxt)

    def edge_fwd(t, carry):
        forward_tile(3 * t)
        return carry

    lax.fori_loop(0, 2, edge_fwd, 0)
    send(a_own, a_par, ps.at[1], pr.at[1], partner)

    for k in range(1, NYL):
        got = pl.multiple_of(((cp + 4) % 8) * 64 + ((yl + NYL - k) % NYL) * 16, 16)
        arrived(wh.at[core, pl.ds(got, 16)], wr.at[3 + k], ws.at[3 + k], partner)
    o_block = wh.at[core, pl.ds(orow, 64)]
    for k in range(1, NX):
        send(o_block, o_block, ws.at[6 + k], wr.at[6 + k], x_peer(k))
    send(o_block, o_block, ps.at[2], pr.at[2], partner)

    arrived(s2p, pr.at[0], ps.at[0], partner)
    arrived(a_par, pr.at[1], ps.at[1], partner)
    for c in range(NC):
        cs = slice(c * CW, (c + 1) * CW)
        dw = dot(a_own[...], sg[core, :, cs], CONTRACT_FIRST)
        dw = dw + dot(a_par[...], s2p[:, cs], CONTRACT_FIRST)
        dw = dw.astype(BF)
        for xt in range(NX):
            xs[c, xt, 0:64] = dw[64 * xt:64 * xt + 64]
            xs[c, xt, 64:128] = dw[256 + 64 * xt:256 + 64 * xt + 64]
        for k in (2, 1, 3):
            send(xs.at[c, (x + k) % NX], xr.at[c, k], xss.at[c, k], xrs.at[c, k], x_peer(k))

    for k in range(1, NX):
        got = pl.multiple_of((yh * NX + (x + NX - k) % NX) * 64, 64)
        block = wh.at[core, pl.ds(got, 64)]
        arrived(block, wr.at[k], ws.at[k], partner)
        send(block, block, ps.at[2 + k], pr.at[2 + k], partner)
    for k in range(1, NX):
        got = pl.multiple_of(((1 - yh) * NX + (x + NX - k) % NX) * 64, 64)
        block = wh.at[core, pl.ds(got, 64)]
        arrived(block, wr.at[6 + k], ws.at[6 + k], partner)
        send(block, block, ps.at[5 + k], pr.at[5 + k], partner)
    loads[4].wait()
    loads[5].wait()
    loads[6].wait()
    any_block = wh.at[1 - core, pl.ds(orow, 64)]
    arrived(any_block, pr.at[2], ps.at[2], partner)
    for k in range(1, NX):
        got = pl.multiple_of((yh * NX + (x + NX - k) % NX) * 64, 64)
        arrived(wh.at[1 - core, pl.ds(got, 64)], pr.at[2 + k], ps.at[2 + k], partner)
    for k in range(1, NX):
        got = pl.multiple_of(((1 - yh) * NX + (x + NX - k) % NX) * 64, 64)
        arrived(wh.at[1 - core, pl.ds(got, 64)], pr.at[5 + k], ps.at[5 + k], partner)

    def tap_chunk(m, carry):
        at = pl.ds(pl.multiple_of((m % 2) * 256, 256), 256)
        proj = dot(a_own[...], wh[m // 2, :, at], PLAIN)
        for u in range(2):
            n = 2 * m + u
            lanes = pl.ds(pl.multiple_of(n * 128, 128), 128)
            mixed = (sbuf[:, lanes].astype(F32) + proj[:, 128 * u:128 * u + 128]) * t_valid
            rows = [
                jnp.sum(mixed * gf[n, pl.ds(19 - j, ROWS), :], axis=0, keepdims=True)
                for j in range(KW)
            ]
            rows.append(jnp.zeros((1, 128), F32))
            cpart[n] = jnp.concatenate(rows, axis=0)
        return carry

    lax.fori_loop(0, 4, tap_chunk, 0)
    c_mine = pl.multiple_of(4 * core, 4)
    c_other = pl.multiple_of(4 * (1 - core), 4)
    send(cpart.at[pl.ds(c_other, 4)], cpr, css.at[0], crs.at[0], partner)

    def x_sum(c):
        total = xs[c, x].astype(F32)
        for k in range(1, NX):
            arrived(xr.at[c, k], xrs.at[c, k], xss.at[c, k], partner)
            total = total + xr[c, k].astype(F32)
        ys[c] = total.astype(BF).reshape(NY, 16, CW)
        for k in (4, 3, 5, 2, 6, 1, 7):
            send(ys.at[c, (y + k) % NY], yr.at[c, k], yss.at[c, k], yrs.at[c, k], y_peer(k))

    for c in range(NC):
        x_sum(c)

    grad_att = dot(sg[0], wh[0], CONTRACT_LAST) + dot(sg[1], wh[1], CONTRACT_LAST)
    ag[...] = grad_att.astype(BF)
    kgacc[...] = jnp.zeros((EXT, HD), F32)
    vgacc[...] = jnp.zeros((EXT, HD), F32)

    def backward_tile(i):
        r0 = pl.multiple_of(i * QT, 16)
        for g in range(2):
            cols = slice(256 * g, 256 * g + 256)
            kk = kext[pl.ds(r0, KT), cols]
            vv = vext[pl.ds(r0, KT), cols]
            qs = stacked(qbuf[pl.ds(r0, QT), cols])
            gs = stacked(ag[pl.ds(r0, QT), cols])
            p = psave[i, g]
            dprob = dot(gs, vv, CONTRACT_LAST)
            inner = jnp.sum(p * dprob, axis=1, keepdims=True)
            ds = (p * (dprob - inner)).astype(BF)
            qg_v[pl.ds(r0, QT), cols] = (unstacked(dot(ds, kk, PLAIN)) * SCALE).astype(BF)
            at = pl.ds(r0, KT)
            kgacc[at, cols] = kgacc[at, cols] + dot(ds, qs, CONTRACT_FIRST)
            vgacc[at, cols] = vgacc[at, cols] + dot(p.astype(BF), gs, CONTRACT_FIRST)

    def edge_bwd(t, carry):
        backward_tile(3 * t)
        return carry

    lax.fori_loop(0, 2, edge_bwd, 0)
    to_prev[0] = (kgacc[0:48] * SCALE).astype(BF)
    to_prev[1] = vgacc[0:48].astype(BF)
    to_next[0] = (kgacc[240:272] * SCALE).astype(BF)
    to_next[1] = vgacc[240:272].astype(BF)
    send(to_prev, from_next, hs.at[6], hr.at[6], prv)
    send(to_next, from_prev, hs.at[7], hr.at[7], nxt)

    arrived(cpr, crs.at[0], css.at[0], partner)
    csx[...] = cpart[pl.ds(c_mine, 4)] + cpr[...]
    for k in range(1, NX):
        send(csx.at[(x + k) % NX], cxr.at[k], css.at[k], crs.at[k], x_peer(k))

    def y_sum(c):
        total = ys[c, y].astype(F32)
        for k in range(1, NY):
            arrived(yr.at[c, k], yrs.at[c, k], yss.at[c, k], partner)
            total = total + yr[c, k].astype(F32)
        zr[c, z] = total.astype(BF)
        for k in (4, 3, 5, 2, 6, 1, 7):
            send(zr.at[c, z], zr.at[c, z], zss.at[c, k], zrs.at[c, k], z_peer(k))

    for c in range(NC):
        y_sum(c)

    def inner_bwd(t, carry):
        backward_tile(1 + t)
        return carry

    lax.fori_loop(0, 2, inner_bwd, 0)
    outs.append(pltpu.make_async_copy(qg_v, qg_out.at[0], out_sem.at[2]))
    outs[-1].start()

    total = csx[x]
    for k in range(1, NX):
        arrived(cxr.at[k], crs.at[k], css.at[k], partner)
        total = total + cxr[k]
    cy[y] = total
    for k in range(1, NY):
        send(cy.at[y], cy.at[y], css.at[3 + k], crs.at[3 + k], y_peer(k))

    arrived(from_next, hr.at[6], hs.at[6], prv)
    arrived(from_prev, hr.at[7], hs.at[7], prv)
    for src, acc, dst, scale in ((0, kgacc, kg_v, SCALE), (1, vgacc, vg_v, 1.0)):
        dst[0:32] = (acc[48:80] * scale + from_prev[src].astype(F32)).astype(BF)
        dst[32:144] = (acc[80:192] * scale).astype(BF)
        dst[144:192] = (acc[192:240] * scale + from_next[src].astype(F32)).astype(BF)
    outs.append(pltpu.make_async_copy(kg_v, kg_out.at[0], out_sem.at[3]))
    outs[-1].start()
    outs.append(pltpu.make_async_copy(vg_v, vg_out.at[0], out_sem.at[4]))
    outs[-1].start()

    def z_sum(c):
        for k in range(1, NZ):
            arrived(zr.at[c, (z + NZ - k) % NZ], zrs.at[c, k], zss.at[c, k], partner)
        total = zr[c, 0].astype(F32)
        for s in range(1, NZ):
            total = total + zr[c, s].astype(F32)
        fin[core, c, pl.ds(ylrow, 16)] = total.astype(BF)
        mine = fin.at[core, c, pl.ds(ylrow, 16)]
        for k in (2, 1, 3):
            send(mine, mine, fss.at[c, k], frs.at[c, k], yl_peer(k))

    for c in range(NC):
        z_sum(c)

    for k in range(1, NY):
        arrived(cy.at[(y + NY - k) % NY], crs.at[3 + k], css.at[3 + k], partner)
    total = cy[0]
    for s in range(1, NY):
        total = total + cy[s]
    cz[z] = total
    for k in range(1, NZ):
        send(cz.at[z], cz.at[z], css.at[10 + k], crs.at[10 + k], z_peer(k))

    for c in range(NC):
        for k in range(1, NYL):
            got = pl.multiple_of(((yl + NYL - k) % NYL) * 16, 16)
            arrived(fin.at[core, c, pl.ds(got, 16)], frs.at[c, k], fss.at[c, k], partner)
        send(fin.at[core, c], fin.at[core, c], fss.at[c, 0], frs.at[c, 0], partner)

    for k in range(1, NZ):
        arrived(cz.at[(z + NZ - k) % NZ], crs.at[10 + k], css.at[10 + k], partner)
    total = cz[0]
    for s in range(1, NZ):
        total = total + cz[s]
    cx[core, x] = total
    for k in range(1, NX):
        send(cx.at[core, x], cx.at[core, x], css.at[17 + k], crs.at[17 + k], x_peer(k))

    for c in range(NC):
        arrived(fin.at[1 - core, c], frs.at[c, 0], fss.at[c, 0], partner)
    for h in range(2):
        for c in range(NC):
            at = h * HALF + c * CW
            wg_v[:, at:at + CW] = fin[h, c].astype(F32)
    outs.append(pltpu.make_async_copy(wg_v, wg_out, out_sem.at[5]))
    outs[-1].start()

    for k in range(1, NX):
        arrived(cx.at[core, (x + NX - k) % NX], crs.at[17 + k], css.at[17 + k], partner)
    send(cx.at[core], cx.at[core], css.at[21], crs.at[21], partner)
    arrived(cx.at[1 - core], crs.at[21], css.at[21], partner)
    for h in range(2):
        for b in range(NX):
            at = h * HALF + b * 128
            cg_v[:, at:at + 128] = cx[h, b, 0:KW]
    outs.append(pltpu.make_async_copy(cg_v, cg_out, out_sem.at[6]))
    outs[-1].start()

    for c in sent:
        c.wait_send()
    for c in outs:
        c.wait()


def body(
    queries, key_rows, value_rows, stream_in, out_grad, out_weight, conv_weight, lengths, offsets
):
    hbm = pl.BlockSpec(memory_space=pltpu.HBM)
    free = pl.BlockSpec(memory_space=pl.ANY)
    smem = pl.BlockSpec(memory_space=pltpu.SMEM)
    vmem = pl.BlockSpec(memory_space=pltpu.VMEM)
    dma = pltpu.SemaphoreType.DMA
    sds = jax.ShapeDtypeStruct
    V = pltpu.VMEM
    return pl.pallas_call(
        kernel,
        in_specs=[smem, smem] + [hbm] * 6 + [vmem],
        out_specs=[free] * 6,
        out_shape=[
            sds((1, ROWS, HD), BF), sds((1, ROWS, HD), BF), sds((1, ROWS, HD), BF),
            sds((1, ROWS, D), BF), sds((64, D), F32), sds((KW, D), F32),
        ],
        scratch_shapes=[
            V((EXT, HD), BF), V((EXT, HD), BF), V((ROWS, HD), BF), V((ROWS, D), BF),
            V((GEXT, D), BF), V((8, GEXT, 128), F32), V((2, HD, HALF), BF),
            V((ROWS, HD), BF), V((ROWS, HD), BF), V((2, ROWS, HALF), BF), V((ROWS, HALF), BF),
            V((ROWS, HD), BF), V((4, 2, 4 * QT, KT), F32),
            V((EXT, HD), F32), V((EXT, HD), F32),
            V((2, 48, HD), BF), V((2, 32, HD), BF), V((2, 48, HD), BF), V((2, 32, HD), BF),
            V((ROWS, HD), BF), V((ROWS, HD), BF), V((ROWS, HD), BF), V((64, D), F32), V((KW, D), F32),
            V((NC, NX, 128, CW), BF), V((NC, NX, 128, CW), BF),
            V((NC, NY, 16, CW), BF), V((NC, NY, 16, CW), BF), V((NC, NZ, 16, CW), BF),
            V((2, NC, 64, CW), BF),
            V((8, 8, 128), F32), V((4, 8, 128), F32), V((4, 8, 128), F32), V((4, 8, 128), F32),
            V((NY, 8, 128), F32), V((NZ, 8, 128), F32), V((2, NX, 8, 128), F32),
            dma((7,)), dma((7,)), dma((8,)), dma((8,)), dma((10,)), dma((10,)), dma((9,)), dma((9,)),
            dma((NC, NX)), dma((NC, NX)), dma((NC, NY)), dma((NC, NY)), dma((NC, NZ)), dma((NC, NZ)),
            dma((NC, NYL)), dma((NC, NYL)), dma((22,)), dma((22,)),
        ],
        compiler_params=pltpu.CompilerParams(
            collective_id=0, has_side_effects=True, vmem_limit_bytes=48 * 1024 * 1024
        ),
        name="fused_backward",
    )(lengths, offsets, queries, key_rows, value_rows, stream_in, out_grad, out_weight, conv_weight)


def solution(mesh):
    row = P("dp", "cp", None)
    return jax.shard_map(
        body,
        mesh=mesh,
        in_specs=(row, row, row, row, row, P("cp", None), P(), P("dp"), P("dp", None)),
        out_specs=(row, row, row, row, P("cp", None), P()),
        check_vma=False,
    )
```

```python
import jax
import jax.numpy as jnp
from jax import lax
from jax.experimental import pallas as pl
from jax.experimental.pallas import tpu as pltpu
from jax.sharding import PartitionSpec as P

HSZ = 64
BLK = 24
KW = 7
ROWS = 192
HD = 512
D = 1024
HALF = 512
NX, NY, NYL, NZ = 4, 8, 4, 8
NC = 2
CW = HALF // NC
QT = 48
KT = 128
EXT = 272
GEXT = 208
NEG = -1e30
SCALE = HSZ ** -0.5
BF = jnp.bfloat16
F32 = jnp.float32
MESH = pl.DeviceIdType.MESH

CONTRACT_LAST = (((1,), (1,)), ((), ()))
CONTRACT_FIRST = (((0,), (0,)), ((), ()))
PLAIN = (((1,), (0,)), ((), ()))


def dot(a, b, dims):
    return lax.dot_general(a, b, dims, preferred_element_type=F32)


def kernel(
    len_ref, off_in, q_in, k_in, v_in, s_in, g_in, w_in, cw_in,
    qg_out, kg_out, vg_out, sg_out, wg_out, cg_out,
    off_ref, cw_ref, kext, vext, vrel, qbuf, sbuf, gext, gf, wh, a_own, a_par, sg, s2p, ag, psave,
    kgacc, vgacc, to_prev, to_next, from_next, from_prev, rel_prev, rel_next,
    qg_v, kg_v, vg_v, wg_v, cg_v,
    xs, xr, xc, xrel, ys, yr, zr, fin,
    cpart, cpr, csx, cxr, cy, cz, cx,
    loc, out_sem, hs, hr, ws, wr, ps, pr, xss, xrs, yss, yrs, zss, zrs, fss, frs, css, crs,
):
    cp = lax.axis_index("cp")
    dp = lax.axis_index("dp")
    yh = cp // NX
    x = cp % NX
    core = dp % 2
    z = (dp // 2) % NZ
    yl = dp // (2 * NZ)
    y = yh * NYL + yl

    def dev(y_to, x_to, z_to, core_to):
        return {
            "cp": (y_to // NYL) * NX + x_to,
            "dp": ((y_to % NYL) * NZ + z_to) * 2 + core_to,
        }

    def x_peer(k, to_core=None):
        return dev(y, (x + k) % NX, z, core if to_core is None else to_core)

    def y_peer(k):
        return dev((y + k) % NY, x, z, core)

    def z_peer(k):
        return dev(y, x, (z + k) % NZ, core)

    def yl_peer(k):
        return dev(yh * NYL + (yl + k) % NYL, x, z, core)

    partner = dev(y, x, z, 1 - core)

    def cp_peer(k):
        return {"cp": (cp + k) % 8, "dp": dp}

    nxt, prv, across = cp_peer(1), cp_peer(7), cp_peer(4)

    def rc(src, dst, ssem, rsem, to):
        return pltpu.make_async_remote_copy(
            src_ref=src, dst_ref=dst, send_sem=ssem, recv_sem=rsem,
            device_id=to, device_id_type=MESH,
        )

    sent = []
    sent_if = []

    def send(src, dst, ssem, rsem, to):
        c = rc(src, dst, ssem, rsem, to)
        c.start()
        sent.append(c)

    def send_if(cond, src, dst, ssem, rsem, to):
        c = rc(src, dst, ssem, rsem, to)
        pl.when(cond)(c.start)
        sent_if.append((cond, c))

    def arrived(dst, rsem, ssem, to):
        rc(dst, dst, ssem, rsem, to).wait_recv()

    def arrived_if(cond, dst, rsem, ssem, to):
        pl.when(cond)(rc(dst, dst, ssem, rsem, to).wait_recv)

    barrier = pltpu.get_barrier_semaphore()
    greet = [y_peer(k) for k in (4, 3, 5, 2, 6, 1, 7)]
    greet += [z_peer(k) for k in (4, 3, 5, 2, 6, 1, 7)]
    greet += [nxt, prv] + [x_peer(k) for k in (2, 1, 3)] + [partner]
    greet += [x_peer(k, 1 - core) for k in (2, 1, 3)] + [cp_peer(3), cp_peer(5)]
    for to in greet:
        pl.semaphore_signal(barrier, inc=1, device_id=to, device_id_type=MESH)

    c512 = pl.multiple_of(core * HALF, HALF)
    cprow = pl.multiple_of(cp * 64, 64)
    orow = pl.multiple_of(((cp + 4) % 8) * 64, 64)
    ylrow = pl.multiple_of(yl * 16, 16)
    wq_mine = pl.multiple_of(cp * 64 + yl * 16, 16)
    wq_other = pl.multiple_of(((cp + 4) % 8) * 64 + yl * 16, 16)

    loads = [
        pltpu.make_async_copy(k_in.at[0], kext.at[pl.ds(48, ROWS)], loc.at[0]),
        pltpu.make_async_copy(q_in.at[0], qbuf, loc.at[1]),
        pltpu.make_async_copy(v_in.at[0], vext.at[pl.ds(48, ROWS)], loc.at[2]),
        pltpu.make_async_copy(g_in.at[0], gext.at[pl.ds(8, ROWS)], loc.at[3]),
        pltpu.make_async_copy(w_in.at[:, pl.ds(0, HALF)], wh.at[0, pl.ds(cprow, 64)], loc.at[4]),
        pltpu.make_async_copy(w_in.at[:, pl.ds(HALF, HALF)], wh.at[1, pl.ds(cprow, 64)], loc.at[5]),
        pltpu.make_async_copy(s_in.at[0], sbuf, loc.at[6]),
        pltpu.make_async_copy(off_in, off_ref, loc.at[7]),
        pltpu.make_async_copy(cw_in, cw_ref, loc.at[8]),
    ]
    for n in (7, 0, 1, 2, 3, 8, 4, 5, 6):
        loads[n].start()

    has_prev = cp > 0
    has_next = cp < 7
    kext[264:272] = jnp.zeros((8, HD), BF)
    vext[264:272] = jnp.zeros((8, HD), BF)
    to_clear = jnp.zeros((48, HD), BF)

    @pl.when(cp == 0)
    def _():
        kext[0:48] = to_clear
        vext[0:48] = to_clear
        gext[0:8] = jnp.zeros((8, D), BF)
        from_prev[...] = jnp.zeros((2, BLK, HD), BF)

    @pl.when(cp == 7)
    def _():
        kext[240:264] = to_clear[0:BLK]
        vext[240:264] = to_clear[0:BLK]
        gext[200:208] = jnp.zeros((8, D), BF)
        from_next[...] = jnp.zeros((2, 48, HD), BF)

    loads[7].wait()
    length = len_ref[0]
    back = off_ref[0, 0]
    ahead = off_ref[0, 1]
    lane = lax.broadcasted_iota(jnp.int32, (1, 256), 1)
    head_f = [((lane // HSZ) == h).astype(F32) for h in range(4)]
    head_b = [m.astype(BF) for m in head_f]
    row_i = lax.broadcasted_iota(jnp.int32, (4 * QT, KT), 0)
    col_i = lax.broadcasted_iota(jnp.int32, (4 * QT, KT), 1)
    rel = col_i // BLK - 2 - (row_i % QT) // BLK
    reach = (rel >= -back) & (rel <= ahead)

    def stacked(block):
        return jnp.concatenate([block * head_b[h] for h in range(4)], axis=0)

    def unstacked(block):
        total = block[0:QT] * head_f[0]
        for h in range(1, 4):
            total = total + block[h * QT:(h + 1) * QT] * head_f[h]
        return total

    def forward_tile(i):
        r0 = pl.multiple_of(i * QT, 16)
        key_frame = cp * ROWS + i * QT - 2 * BLK + col_i
        ok = reach & (key_frame >= 0) & (key_frame < length)
        frame = cp * ROWS + i * QT + lax.broadcasted_iota(jnp.int32, (QT, 1), 0)
        valid = (frame < length).astype(F32)
        for g in range(2):
            cols = slice(256 * g, 256 * g + 256)
            kk = kext[pl.ds(r0, KT), cols]
            vv = vext[pl.ds(r0, KT), cols]
            qs = stacked(qbuf[pl.ds(r0, QT), cols])
            s = jnp.where(ok, dot(qs, kk, CONTRACT_LAST) * SCALE, NEG)
            e = jnp.exp(s - jnp.max(s, axis=1, keepdims=True))
            p = e / jnp.sum(e, axis=1, keepdims=True)
            psave[i, g] = p
            o = unstacked(dot(p.astype(BF), vv, PLAIN))
            a_own[pl.ds(r0, QT), cols] = (o * valid).astype(BF)

    for n in (0, 1, 2):
        loads[n].wait()

    def inner_fwd(t, carry):
        forward_tile(1 + t)
        return carry

    lax.fori_loop(0, 2, inner_fwd, 0)

    pl.semaphore_wait(barrier, len(greet))

    gi, ki, vi = g_in.at[0], k_in.at[0], v_in.at[0]
    k_lo, k_hi = kext.at[pl.ds(0, 48)], kext.at[pl.ds(240, BLK)]
    v_lo, v_hi = vext.at[pl.ds(0, 48)], vext.at[pl.ds(240, BLK)]
    g_lo, g_hi = gext.at[pl.ds(0, 8)], gext.at[pl.ds(200, 8)]
    send_if(has_next, gi.at[pl.ds(184, 8)], g_lo, hs.at[0], hr.at[0], nxt)
    send_if(has_prev, gi.at[pl.ds(0, 8)], g_hi, hs.at[1], hr.at[1], prv)
    send(
        w_in.at[pl.ds(ylrow, 16), pl.ds(c512, HALF)],
        wh.at[core, pl.ds(wq_mine, 16)], ws.at[0], wr.at[0], across,
    )
    v_last, v_first = vi.at[pl.ds(144, 48)], vi.at[pl.ds(0, BLK)]
    send_if(cp == 3, v_last, vrel, hs.at[8], hr.at[8], across)
    send_if(cp == 4, v_first, vrel.at[pl.ds(0, BLK)], hs.at[8], hr.at[8], across)
    send_if(has_next, ki.at[pl.ds(144, 48)], k_lo, hs.at[2], hr.at[2], nxt)
    send_if(has_prev, ki.at[pl.ds(0, BLK)], k_hi, hs.at[3], hr.at[3], prv)
    send_if(has_next & (cp != 3), v_last, v_lo, hs.at[4], hr.at[4], nxt)
    send_if(has_prev & (cp != 4), v_first, v_hi, hs.at[5], hr.at[5], prv)
    for k in range(1, NX):
        send(
            w_in.at[:, pl.ds(c512, HALF)],
            wh.at[core, pl.ds(cprow, 64)], ws.at[k], wr.at[k], x_peer(k),
        )

    loads[3].wait()
    loads[8].wait()

    def tap_sum(n, lanes, r0, r1):
        acc = jnp.zeros((r1 - r0, 128), F32)
        for j in range(KW):
            acc = acc + cw_ref[pl.ds(j, 1), lanes] * gf[n, pl.ds(r0 + 11 - j, r1 - r0), :]
        frame = cp * ROWS + r0 + lax.broadcasted_iota(jnp.int32, (r1 - r0, 128), 0)
        at = pl.ds(pl.multiple_of((n % 4) * 128, 128), 128)
        sg[n // 4, r0:r1, at] = jnp.where(frame < length, acc, 0.0).astype(BF)

    def masked_rows(n, lanes, r0, r1):
        frame = cp * ROWS - 8 + r0 + lax.broadcasted_iota(jnp.int32, (r1 - r0, 128), 0)
        ok = (frame >= 0) & (frame < length)
        gf[n, r0:r1] = jnp.where(ok, gext[r0:r1, lanes].astype(F32), 0.0)

    def conv_inside(n, carry):
        lanes = pl.ds(pl.multiple_of(n * 128, 128), 128)
        masked_rows(n, lanes, 8, 200)
        tap_sum(n, lanes, 16, 176)
        return carry

    def conv_edges(n, carry):
        lanes = pl.ds(pl.multiple_of(n * 128, 128), 128)
        masked_rows(n, lanes, 0, 8)
        masked_rows(n, lanes, 200, 208)
        tap_sum(n, lanes, 0, 16)
        tap_sum(n, lanes, 176, 192)
        return carry

    lax.fori_loop(0, 8, conv_inside, 0)

    arrived_if(has_prev, g_lo, hr.at[0], hs.at[0], nxt)
    arrived_if(has_next, g_hi, hr.at[1], hs.at[1], nxt)

    lax.fori_loop(0, 8, conv_edges, 0)
    send(sg.at[1 - core], s2p, ps.at[0], pr.at[0], partner)
    outs = [
        pltpu.make_async_copy(sg.at[0], sg_out.at[0, :, pl.ds(0, HALF)], out_sem.at[0]),
        pltpu.make_async_copy(sg.at[1], sg_out.at[0, :, pl.ds(HALF, HALF)], out_sem.at[1]),
    ]
    outs[0].start()
    outs[1].start()

    quarter = wh.at[core, pl.ds(wq_other, 16)]
    arrived(quarter, wr.at[0], ws.at[0], across)
    for k in range(1, NYL):
        send(quarter, quarter, ws.at[3 + k], wr.at[3 + k], yl_peer(k))

    arrived_if(cp == 7, vrel, hr.at[8], hs.at[8], across)
    send_if(cp == 7, vrel, v_lo, hs.at[4], hr.at[4], cp_peer(5))
    arrived_if(cp == 0, vrel.at[pl.ds(0, BLK)], hr.at[8], hs.at[8], across)
    send_if(cp == 0, vrel.at[pl.ds(0, BLK)], v_hi, hs.at[5], hr.at[5], cp_peer(3))
    for k in range(1, NX):
        got = pl.multiple_of((yh * NX + (x + NX - k) % NX) * 64, 64)
        block = wh.at[core, pl.ds(got, 64)]
        arrived(block, wr.at[k], ws.at[k], partner)
        send(block, block, ps.at[2 + k], pr.at[2 + k], partner)

    arrived_if(has_prev, k_lo, hr.at[2], hs.at[2], nxt)
    arrived_if(has_next, k_hi, hr.at[3], hs.at[3], nxt)
    arrived_if(has_prev, v_lo, hr.at[4], hs.at[4], nxt)
    arrived_if(has_next, v_hi, hr.at[5], hs.at[5], nxt)

    def edge_fwd(t, carry):
        forward_tile(3 * t)
        return carry

    lax.fori_loop(0, 2, edge_fwd, 0)
    send(a_own, a_par, ps.at[1], pr.at[1], partner)

    for k in range(1, NYL):
        got = pl.multiple_of(((cp + 4) % 8) * 64 + ((yl + NYL - k) % NYL) * 16, 16)
        arrived(wh.at[core, pl.ds(got, 16)], wr.at[3 + k], ws.at[3 + k], partner)
    o_block = wh.at[core, pl.ds(orow, 64)]
    for k in range(1, NX):
        send(o_block, o_block, ws.at[6 + k], wr.at[6 + k], x_peer(k))
    send(o_block, o_block, ps.at[2], pr.at[2], partner)

    arrived(s2p, pr.at[0], ps.at[0], partner)
    arrived(a_par, pr.at[1], ps.at[1], partner)

    low, high = pl.ds(0, 64), pl.ds(64, 64)
    for c in range(NC):
        cs = slice(c * CW, (c + 1) * CW)
        dw = dot(a_own[...], sg[core, :, cs], CONTRACT_FIRST)
        dw = dw + dot(a_par[...], s2p[:, cs], CONTRACT_FIRST)
        dw = dw.astype(BF)
        for xt in range(NX):
            xs[c, xt, 0:64] = dw[64 * xt:64 * xt + 64]
            xs[c, xt, 64:128] = dw[256 + 64 * xt:256 + 64 * xt + 64]
        far = (x + 2) % NX
        send(xs.at[c, far, low], xrel.at[c, 0], xss.at[c, 0], xrs.at[c, 0], x_peer(1))
        send(xs.at[c, far, high], xrel.at[c, 1], xss.at[c, 1], xrs.at[c, 1], x_peer(3))
        send(xs.at[c, (x + 1) % NX, high], xr.at[c, 0, high], xss.at[c, 2], xrs.at[c, 2], x_peer(1))
        send(xs.at[c, (x + 3) % NX, low], xr.at[c, 1, low], xss.at[c, 3], xrs.at[c, 3], x_peer(3))

    for c in range(NC):
        arrived(xrel.at[c, 0], xrs.at[c, 0], xss.at[c, 0], partner)
        xc[c, 0] = (xs[c, (x + 1) % NX, 0:64].astype(F32) + xrel[c, 0].astype(F32)).astype(BF)
        send(xc.at[c, 0], xr.at[c, 0, low], xss.at[c, 4], xrs.at[c, 4], x_peer(1))
        arrived(xrel.at[c, 1], xrs.at[c, 1], xss.at[c, 1], partner)
        xc[c, 1] = (xs[c, (x + 3) % NX, 64:128].astype(F32) + xrel[c, 1].astype(F32)).astype(BF)
        send(xc.at[c, 1], xr.at[c, 1, high], xss.at[c, 5], xrs.at[c, 5], x_peer(3))

    for k in range(1, NX):
        got = pl.multiple_of(((1 - yh) * NX + (x + NX - k) % NX) * 64, 64)
        block = wh.at[core, pl.ds(got, 64)]
        arrived(block, wr.at[6 + k], ws.at[6 + k], partner)
        send(block, block, ps.at[5 + k], pr.at[5 + k], partner)
    loads[4].wait()
    loads[5].wait()
    loads[6].wait()
    arrived(wh.at[1 - core, pl.ds(orow, 64)], pr.at[2], ps.at[2], partner)
    for k in range(1, NX):
        got = pl.multiple_of((yh * NX + (x + NX - k) % NX) * 64, 64)
        arrived(wh.at[1 - core, pl.ds(got, 64)], pr.at[2 + k], ps.at[2 + k], partner)
    for k in range(1, NX):
        got = pl.multiple_of(((1 - yh) * NX + (x + NX - k) % NX) * 64, 64)
        arrived(wh.at[1 - core, pl.ds(got, 64)], pr.at[5 + k], ps.at[5 + k], partner)

    t_frame = cp * ROWS + lax.broadcasted_iota(jnp.int32, (ROWS, 128), 0)
    t_valid = (t_frame < length).astype(F32)

    def tap_chunk(m, carry):
        at = pl.ds(pl.multiple_of((m % 2) * 256, 256), 256)
        proj = dot(a_own[...], wh[m // 2, :, at], PLAIN)
        for u in range(2):
            n = 2 * m + u
            lanes = pl.ds(pl.multiple_of(n * 128, 128), 128)
            mixed = (sbuf[:, lanes].astype(F32) + proj[:, 128 * u:128 * u + 128]) * t_valid
            rows = [
                jnp.sum(mixed * gf[n, pl.ds(11 - j, ROWS), :], axis=0, keepdims=True)
                for j in range(KW)
            ]
            rows.append(jnp.zeros((1, 128), F32))
            cpart[n] = jnp.concatenate(rows, axis=0)
        return carry

    lax.fori_loop(0, 4, tap_chunk, 0)
    c_mine = pl.multiple_of(4 * core, 4)
    c_other = pl.multiple_of(4 * (1 - core), 4)
    send(cpart.at[pl.ds(c_other, 4)], cpr, css.at[0], crs.at[0], partner)

    def x_sum(c):
        arrived(xr.at[c, 0, high], xrs.at[c, 2], xss.at[c, 2], partner)
        arrived(xr.at[c, 1, low], xrs.at[c, 3], xss.at[c, 3], partner)
        arrived(xr.at[c, 0, low], xrs.at[c, 4], xss.at[c, 4], partner)
        arrived(xr.at[c, 1, high], xrs.at[c, 5], xss.at[c, 5], partner)
        total = xs[c, x].astype(F32) + xr[c, 0].astype(F32) + xr[c, 1].astype(F32)
        ys[c] = total.astype(BF).reshape(NY, 16, CW)
        for k in (4, 3, 5, 2, 6, 1, 7):
            send(ys.at[c, (y + k) % NY], yr.at[c, k], yss.at[c, k], yrs.at[c, k], y_peer(k))

    for c in range(NC):
        x_sum(c)

    arrived(cpr, crs.at[0], css.at[0], partner)
    csx[...] = cpart[pl.ds(c_mine, 4)] + cpr[...]
    for k in range(1, NX):
        send(csx.at[(x + k) % NX], cxr.at[k], css.at[k], crs.at[k], x_peer(k))

    grad_att = dot(sg[0], wh[0], CONTRACT_LAST) + dot(sg[1], wh[1], CONTRACT_LAST)
    ag[...] = grad_att.astype(BF)
    kgacc[...] = jnp.zeros((EXT, HD), F32)
    vgacc[...] = jnp.zeros((EXT, HD), F32)

    def backward_tile(i):
        r0 = pl.multiple_of(i * QT, 16)
        for g in range(2):
            cols = slice(256 * g, 256 * g + 256)
            kk = kext[pl.ds(r0, KT), cols]
            vv = vext[pl.ds(r0, KT), cols]
            qs = stacked(qbuf[pl.ds(r0, QT), cols])
            gs = stacked(ag[pl.ds(r0, QT), cols])
            p = psave[i, g]
            dprob = dot(gs, vv, CONTRACT_LAST)
            inner = jnp.sum(p * dprob, axis=1, keepdims=True)
            ds = (p * (dprob - inner)).astype(BF)
            qg_v[pl.ds(r0, QT), cols] = (unstacked(dot(ds, kk, PLAIN)) * SCALE).astype(BF)
            at = pl.ds(r0, KT)
            kgacc[at, cols] = kgacc[at, cols] + dot(ds, qs, CONTRACT_FIRST)
            vgacc[at, cols] = vgacc[at, cols] + dot(p.astype(BF), gs, CONTRACT_FIRST)

    def edge_bwd(t, carry):
        backward_tile(3 * t)
        return carry

    lax.fori_loop(0, 2, edge_bwd, 0)
    to_prev[0] = (kgacc[0:48] * SCALE).astype(BF)
    to_prev[1] = vgacc[0:48].astype(BF)
    to_next[0] = (kgacc[240:264] * SCALE).astype(BF)
    to_next[1] = vgacc[240:264].astype(BF)

    total = csx[x]
    for k in range(1, NX):
        arrived(cxr.at[k], crs.at[k], css.at[k], partner)
        total = total + cxr[k]
    cy[y] = total
    for k in range(1, NY):
        send(cy.at[y], cy.at[y], css.at[3 + k], crs.at[3 + k], y_peer(k))

    def y_sum(c):
        total = ys[c, y].astype(F32)
        for k in range(1, NY):
            arrived(yr.at[c, k], yrs.at[c, k], yss.at[c, k], partner)
            total = total + yr[c, k].astype(F32)
        zr[c, z] = total.astype(BF)
        for k in (4, 3, 5, 2, 6, 1, 7):
            send(zr.at[c, z], zr.at[c, z], zss.at[c, k], zrs.at[c, k], z_peer(k))

    for c in range(NC):
        y_sum(c)

    send_if(cp == 3, to_next.at[1], rel_next, hs.at[9], hr.at[9], across)
    send_if(cp == 4, to_prev.at[1], rel_prev, hs.at[9], hr.at[9], across)
    send_if(has_prev, to_prev.at[0], from_next.at[0], hs.at[6], hr.at[6], prv)
    send_if(has_next, to_next.at[0], from_prev.at[0], hs.at[7], hr.at[7], nxt)
    send_if(has_prev & (cp != 4), to_prev.at[1], from_next.at[1], hs.at[10], hr.at[10], prv)
    send_if(has_next & (cp != 3), to_next.at[1], from_prev.at[1], hs.at[11], hr.at[11], nxt)

    def inner_bwd(t, carry):
        backward_tile(1 + t)
        return carry

    lax.fori_loop(0, 2, inner_bwd, 0)
    outs.append(pltpu.make_async_copy(qg_v, qg_out.at[0], out_sem.at[2]))
    outs[-1].start()

    for k in range(1, NY):
        arrived(cy.at[(y + NY - k) % NY], crs.at[3 + k], css.at[3 + k], partner)
    total = cy[0]
    for s in range(1, NY):
        total = total + cy[s]
    cz[z] = total
    for k in range(1, NZ):
        send(cz.at[z], cz.at[z], css.at[10 + k], crs.at[10 + k], z_peer(k))

    def z_sum(c):
        for k in range(1, NZ):
            arrived(zr.at[c, (z + NZ - k) % NZ], zrs.at[c, k], zss.at[c, k], partner)
        total = zr[c, 0].astype(F32)
        for s in range(1, NZ):
            total = total + zr[c, s].astype(F32)
        fin[core, c, pl.ds(ylrow, 16)] = total.astype(BF)
        mine = fin.at[core, c, pl.ds(ylrow, 16)]
        for k in (2, 1, 3):
            send(mine, mine, fss.at[c, k], frs.at[c, k], yl_peer(k))

    for c in range(NC):
        z_sum(c)

    arrived_if(cp == 7, rel_next, hr.at[9], hs.at[9], across)
    send_if(cp == 7, rel_next, from_prev.at[1], hs.at[11], hr.at[11], cp_peer(5))
    arrived_if(cp == 0, rel_prev, hr.at[9], hs.at[9], across)
    send_if(cp == 0, rel_prev, from_next.at[1], hs.at[10], hr.at[10], cp_peer(3))

    for k in range(1, NZ):
        arrived(cz.at[(z + NZ - k) % NZ], crs.at[10 + k], css.at[10 + k], partner)
    total = cz[0]
    for s in range(1, NZ):
        total = total + cz[s]
    cx[core, x] = total
    mine = cx.at[core, x]
    for k in range(1, NX):
        send(mine, mine, css.at[17 + k], crs.at[17 + k], x_peer(k))
        send(mine, mine, css.at[20 + k], crs.at[20 + k], x_peer(k, 1 - core))
    send(mine, mine, css.at[24], crs.at[24], partner)

    for c in range(NC):
        for k in range(1, NYL):
            got = pl.multiple_of(((yl + NYL - k) % NYL) * 16, 16)
            arrived(fin.at[core, c, pl.ds(got, 16)], frs.at[c, k], fss.at[c, k], partner)
        send(fin.at[core, c], fin.at[core, c], fss.at[c, 0], frs.at[c, 0], partner)

    arrived_if(has_next, from_next.at[0], hr.at[6], hs.at[6], prv)
    arrived_if(has_prev, from_prev.at[0], hr.at[7], hs.at[7], prv)
    arrived_if(has_next, from_next.at[1], hr.at[10], hs.at[10], prv)
    arrived_if(has_prev, from_prev.at[1], hr.at[11], hs.at[11], prv)
    for src, acc, dst, scale in ((0, kgacc, kg_v, SCALE), (1, vgacc, vg_v, 1.0)):
        low_rows = acc[48:80] * scale
        extra = from_prev[src].astype(F32)
        dst[0:32] = jnp.concatenate([low_rows[0:BLK] + extra, low_rows[BLK:32]], axis=0).astype(BF)
        dst[32:144] = (acc[80:192] * scale).astype(BF)
        dst[144:192] = (acc[192:240] * scale + from_next[src].astype(F32)).astype(BF)
    outs.append(pltpu.make_async_copy(kg_v, kg_out.at[0], out_sem.at[3]))
    outs[-1].start()
    outs.append(pltpu.make_async_copy(vg_v, vg_out.at[0], out_sem.at[4]))
    outs[-1].start()

    for k in range(1, NX):
        from_x = (x + NX - k) % NX
        arrived(cx.at[core, from_x], crs.at[17 + k], css.at[17 + k], partner)
        arrived(cx.at[1 - core, from_x], crs.at[20 + k], css.at[20 + k], partner)
    arrived(cx.at[1 - core, x], crs.at[24], css.at[24], partner)
    for h in range(2):
        for b in range(NX):
            at = h * HALF + b * 128
            cg_v[:, at:at + 128] = cx[h, b, 0:KW]
    outs.append(pltpu.make_async_copy(cg_v, cg_out, out_sem.at[6]))
    outs[-1].start()

    for c in range(NC):
        arrived(fin.at[1 - core, c], frs.at[c, 0], fss.at[c, 0], partner)
    for h in range(2):
        for c in range(NC):
            at = h * HALF + c * CW
            wg_v[:, at:at + CW] = fin[h, c].astype(F32)
    outs.append(pltpu.make_async_copy(wg_v, wg_out, out_sem.at[5]))
    outs[-1].start()

    for c in sent:
        c.wait_send()
    for cond, c in sent_if:
        pl.when(cond)(c.wait_send)
    for c in outs:
        c.wait()


def finish(*refs):
    ins, outs, sem = refs[:6], refs[6:12], refs[12]
    copies = [pltpu.make_async_copy(a, b, sem.at[n]) for n, (a, b) in enumerate(zip(ins, outs))]
    for c in copies:
        c.start()
    for c in copies:
        c.wait()


def body(
    queries, key_rows, value_rows, stream_in, out_grad, out_weight, conv_weight, lengths, offsets
):
    hbm = pl.BlockSpec(memory_space=pltpu.HBM)
    free = pl.BlockSpec(memory_space=pl.ANY)
    dma = pltpu.SemaphoreType.DMA
    sds = jax.ShapeDtypeStruct
    V = pltpu.VMEM
    held = lambda a: pltpu.with_memory_space_constraint(a, pltpu.HBM)
    shapes = [
            sds((1, ROWS, HD), BF), sds((1, ROWS, HD), BF), sds((1, ROWS, HD), BF),
            sds((1, ROWS, D), BF), sds((64, D), F32), sds((KW, D), F32),
        ]
    made = pl.pallas_call(
        kernel,
        in_specs=[pl.BlockSpec(memory_space=pltpu.SMEM)] + [hbm] * 8,
        out_specs=[free] * 6,
        out_shape=shapes,
        scratch_shapes=[
            pltpu.SMEM((1, 2), jnp.int32), V((KW, D), F32),
            V((EXT, HD), BF), V((EXT, HD), BF), V((48, HD), BF), V((ROWS, HD), BF), V((ROWS, D), BF),
            V((GEXT, D), BF), V((8, GEXT, 128), F32), V((2, HD, HALF), BF),
            V((ROWS, HD), BF), V((ROWS, HD), BF), V((2, ROWS, HALF), BF), V((ROWS, HALF), BF),
            V((ROWS, HD), BF), V((4, 2, 4 * QT, KT), F32),
            V((EXT, HD), F32), V((EXT, HD), F32),
            V((2, 48, HD), BF), V((2, BLK, HD), BF), V((2, 48, HD), BF), V((2, BLK, HD), BF),
            V((48, HD), BF), V((BLK, HD), BF),
            V((ROWS, HD), BF), V((ROWS, HD), BF), V((ROWS, HD), BF), V((64, D), F32), V((KW, D), F32),
            V((NC, NX, 128, CW), BF), V((NC, 2, 128, CW), BF), V((NC, 2, 64, CW), BF), V((NC, 2, 64, CW), BF),
            V((NC, NY, 16, CW), BF), V((NC, NY, 16, CW), BF), V((NC, NZ, 16, CW), BF),
            V((2, NC, 64, CW), BF),
            V((8, 8, 128), F32), V((4, 8, 128), F32), V((4, 8, 128), F32), V((4, 8, 128), F32),
            V((NY, 8, 128), F32), V((NZ, 8, 128), F32), V((2, NX, 8, 128), F32),
            dma((9,)), dma((7,)), dma((12,)), dma((12,)), dma((10,)), dma((10,)), dma((9,)), dma((9,)),
            dma((NC, 6)), dma((NC, 6)), dma((NC, NY)), dma((NC, NY)), dma((NC, NZ)), dma((NC, NZ)),
            dma((NC, NYL)), dma((NC, NYL)), dma((25,)), dma((25,)),
        ],
        compiler_params=pltpu.CompilerParams(
            collective_id=0, has_side_effects=True, vmem_limit_bytes=48 * 1024 * 1024
        ),
        name="fused_backward",
    )(lengths, *map(held, (
        offsets, queries, key_rows, value_rows, stream_in, out_grad, out_weight, conv_weight
    )))
    return pl.pallas_call(
        finish,
        in_specs=[free] * 6,
        out_specs=[free] * 6,
        out_shape=shapes,
        scratch_shapes=[dma((6,))],
        compiler_params=pltpu.CompilerParams(vmem_limit_bytes=1024 * 1024),
        name="finish",
    )(*made)


def solution(mesh):
    row = P("dp", "cp", None)
    return jax.shard_map(
        body,
        mesh=mesh,
        in_specs=(row, row, row, row, row, P("cp", None), P(), P("dp"), P("dp", None)),
        out_specs=(row, row, row, row, P("cp", None), P()),
        check_vma=False,
    )
```

```python
import jax
import jax.numpy as jnp
from jax import lax
from jax.experimental import pallas as pl
from jax.experimental.pallas import tpu as pltpu
from jax.sharding import PartitionSpec as P

HSZ = 64
BLK = 24
KW = 7
ROWS = 192
HD = 512
D = 1024
HALF = 512
NX, NY, NYL, NZ = 4, 8, 4, 8
NC = 2
CW = HALF // NC
QT = 48
KT = 128
EXT = 272
GEXT = 208
NEG = -1e30
SCALE = HSZ ** -0.5
BF = jnp.bfloat16
F32 = jnp.float32
MESH = pl.DeviceIdType.MESH
FAR = (4, 3, 5, 2, 6, 1, 7)

CONTRACT_LAST = (((1,), (1,)), ((), ()))
CONTRACT_FIRST = (((0,), (0,)), ((), ()))
PLAIN = (((1,), (0,)), ((), ()))


def dot(a, b, dims):
    return lax.dot_general(a, b, dims, preferred_element_type=F32)


def kernel(
    len_ref, off_in, q_in, k_in, v_in, s_in, g_in, w_in, cw_in,
    qg_out, kg_out, vg_out, sg_out, wg_out, cg_out,
    off_ref, cw_ref, kext, vext, vrel, qbuf, sbuf, gext, gf, wh, a_own, a_par, sg, s2p, ag, psave,
    kgacc, vgacc, to_prev, to_next, from_next, from_prev, rel_prev, rel_next,
    qg_v, kg_v, vg_v, wg_v, cg_v,
    xs, xr, xc, xrel, ys, yr, zr, fin, bs, br, bsum, bz, finb,
    cpart, cxr, cy, cz, cx,
    loc, out_sem, hs, hr, xss, xrs, gs, gr,
):
    cp = lax.axis_index("cp")
    dp = lax.axis_index("dp")
    yh = cp // NX
    x = cp % NX
    core = dp % 2
    z = (dp // 2) % NZ
    yl = dp // (2 * NZ)
    y = yh * NYL + yl

    def dev(y_to, x_to, z_to, core_to):
        return {
            "cp": (y_to // NYL) * NX + x_to,
            "dp": ((y_to % NYL) * NZ + z_to) * 2 + core_to,
        }

    def x_peer(k, to_core=None):
        return dev(y, (x + k) % NX, z, core if to_core is None else to_core)

    def y_peer(k):
        return dev((y + k) % NY, x, z, core)

    def z_peer(k):
        return dev(y, x, (z + k) % NZ, core)

    def yl_peer(k, to_core=None):
        return dev(yh * NYL + (yl + k) % NYL, x, z, core if to_core is None else to_core)

    partner = dev(y, x, z, 1 - core)

    def cp_peer(k):
        return {"cp": (cp + k) % 8, "dp": dp}

    nxt, prv, across = cp_peer(1), cp_peer(7), cp_peer(4)

    def rc(src, dst, ssem, rsem, to):
        return pltpu.make_async_remote_copy(
            src_ref=src, dst_ref=dst, send_sem=ssem, recv_sem=rsem,
            device_id=to, device_id_type=MESH,
        )

    sent = []
    sent_if = []

    def send(src, dst, ssem, rsem, to):
        c = rc(src, dst, ssem, rsem, to)
        c.start()
        sent.append(c)

    def send_if(cond, src, dst, ssem, rsem, to):
        c = rc(src, dst, ssem, rsem, to)
        pl.when(cond)(c.start)
        sent_if.append((cond, c))

    def spread(n, whole, copies):
        for src, dst, to in copies:
            rc(src, dst, gs.at[n], gr.at[n], to).start()
        sent.append(rc(whole, whole, gs.at[n], gr.at[n], partner))

    def landed(n, whole):
        rc(whole, whole, gs.at[n], gr.at[n], partner).wait_recv()

    def arrived(dst, rsem, ssem, to):
        rc(dst, dst, ssem, rsem, to).wait_recv()

    def arrived_if(cond, dst, rsem, ssem, to):
        pl.when(cond)(rc(dst, dst, ssem, rsem, to).wait_recv)

    barrier = pltpu.get_barrier_semaphore()
    greet = [y_peer(k) for k in (4, 3, 5, 2, 6, 1, 7)]
    greet += [z_peer(k) for k in (4, 3, 5, 2, 6, 1, 7)]
    greet += [nxt, prv] + [x_peer(k) for k in (2, 1, 3)] + [partner]
    greet += [yl_peer(k, 1 - core) for k in (2, 1, 3)] + [x_peer(k, 1 - core) for k in (2, 1, 3)] + [cp_peer(3), cp_peer(5)]
    for to in greet:
        pl.semaphore_signal(barrier, inc=1, device_id=to, device_id_type=MESH)

    c512 = pl.multiple_of(core * HALF, HALF)
    cprow = pl.multiple_of(cp * 64, 64)
    orow = pl.multiple_of(((cp + 4) % 8) * 64, 64)
    ylrow = pl.multiple_of(yl * 16, 16)
    wq_mine = pl.multiple_of(cp * 64 + yl * 16, 16)

    loads = [
        pltpu.make_async_copy(k_in.at[0], kext.at[pl.ds(48, ROWS)], loc.at[0]),
        pltpu.make_async_copy(q_in.at[0], qbuf, loc.at[1]),
        pltpu.make_async_copy(v_in.at[0], vext.at[pl.ds(48, ROWS)], loc.at[2]),
        pltpu.make_async_copy(g_in.at[0], gext.at[pl.ds(8, ROWS)], loc.at[3]),
        pltpu.make_async_copy(w_in.at[:, pl.ds(0, HALF)], wh.at[0, pl.ds(cprow, 64)], loc.at[4]),
        pltpu.make_async_copy(w_in.at[:, pl.ds(HALF, HALF)], wh.at[1, pl.ds(cprow, 64)], loc.at[5]),
        pltpu.make_async_copy(s_in.at[0], sbuf, loc.at[6]),
        pltpu.make_async_copy(off_in, off_ref, loc.at[7]),
        pltpu.make_async_copy(cw_in, cw_ref, loc.at[8]),
    ]
    for n in (7, 0, 1, 2, 3, 8, 4, 5, 6):
        loads[n].start()

    has_prev = cp > 0
    has_next = cp < 7
    kext[264:272] = jnp.zeros((8, HD), BF)
    vext[264:272] = jnp.zeros((8, HD), BF)
    to_clear = jnp.zeros((48, HD), BF)

    @pl.when(cp == 0)
    def _():
        kext[0:48] = to_clear
        vext[0:48] = to_clear
        gext[0:8] = jnp.zeros((8, D), BF)
        from_prev[...] = jnp.zeros((2, BLK, HD), BF)

    @pl.when(cp == 7)
    def _():
        kext[240:264] = to_clear[0:BLK]
        vext[240:264] = to_clear[0:BLK]
        gext[200:208] = jnp.zeros((8, D), BF)
        from_next[...] = jnp.zeros((2, 48, HD), BF)

    loads[7].wait()
    length = len_ref[0]
    back = off_ref[0, 0]
    ahead = off_ref[0, 1]
    lane = lax.broadcasted_iota(jnp.int32, (1, 256), 1)
    head_f = [((lane // HSZ) == h).astype(F32) for h in range(4)]
    head_b = [m.astype(BF) for m in head_f]
    row_i = lax.broadcasted_iota(jnp.int32, (4 * QT, KT), 0)
    col_i = lax.broadcasted_iota(jnp.int32, (4 * QT, KT), 1)
    rel = col_i // BLK - 2 - (row_i % QT) // BLK
    reach = (rel >= -back) & (rel <= ahead)

    def stacked(block):
        return jnp.concatenate([block * head_b[h] for h in range(4)], axis=0)

    def unstacked(block):
        total = block[0:QT] * head_f[0]
        for h in range(1, 4):
            total = total + block[h * QT:(h + 1) * QT] * head_f[h]
        return total

    def forward_tile(i):
        r0 = pl.multiple_of(i * QT, 16)
        key_frame = cp * ROWS + i * QT - 2 * BLK + col_i
        ok = reach & (key_frame >= 0) & (key_frame < length)
        frame = cp * ROWS + i * QT + lax.broadcasted_iota(jnp.int32, (QT, 1), 0)
        valid = (frame < length).astype(F32)
        for g in range(2):
            cols = slice(256 * g, 256 * g + 256)
            kk = kext[pl.ds(r0, KT), cols]
            vv = vext[pl.ds(r0, KT), cols]
            qs = stacked(qbuf[pl.ds(r0, QT), cols])
            s = jnp.where(ok, dot(qs, kk, CONTRACT_LAST) * SCALE, NEG)
            e = jnp.exp(s - jnp.max(s, axis=1, keepdims=True))
            p = e / jnp.sum(e, axis=1, keepdims=True)
            psave[i, g] = p
            o = unstacked(dot(p.astype(BF), vv, PLAIN))
            a_own[pl.ds(r0, QT), cols] = (o * valid).astype(BF)

    for n in (0, 1, 2):
        loads[n].wait()

    def inner_fwd(t, carry):
        forward_tile(1 + t)
        return carry

    lax.fori_loop(0, 2, inner_fwd, 0)

    pl.semaphore_wait(barrier, len(greet))

    gi, ki, vi = g_in.at[0], k_in.at[0], v_in.at[0]
    k_lo, k_hi = kext.at[pl.ds(0, 48)], kext.at[pl.ds(240, BLK)]
    v_lo, v_hi = vext.at[pl.ds(0, 48)], vext.at[pl.ds(240, BLK)]
    g_lo, g_hi = gext.at[pl.ds(0, 8)], gext.at[pl.ds(200, 8)]
    send_if(has_next, gi.at[pl.ds(184, 8)], g_lo, hs.at[0], hr.at[0], nxt)
    send_if(has_prev, gi.at[pl.ds(0, 8)], g_hi, hs.at[1], hr.at[1], prv)
    wq = wh.at[core, pl.ds(wq_mine, 16)]
    o_block = wh.at[core, pl.ds(orow, 64)]
    three = wh.at[core, pl.ds(0, 192)]
    spread(12, o_block, [
        (w_in.at[pl.ds(ylrow, 16), pl.ds(c512, HALF)], wq, dev((1 - yh) * NYL + k, x, z, core))
        for k in range(NYL)
    ])
    v_last, v_first = vi.at[pl.ds(144, 48)], vi.at[pl.ds(0, BLK)]
    send_if(cp == 3, v_last, vrel, hs.at[8], hr.at[8], across)
    send_if(cp == 4, v_first, vrel.at[pl.ds(0, BLK)], hs.at[8], hr.at[8], across)
    send_if(has_next, ki.at[pl.ds(144, 48)], k_lo, hs.at[2], hr.at[2], nxt)
    send_if(has_prev, ki.at[pl.ds(0, BLK)], k_hi, hs.at[3], hr.at[3], prv)
    send_if(has_next & (cp != 3), v_last, v_lo, hs.at[4], hr.at[4], nxt)
    send_if(has_prev & (cp != 4), v_first, v_hi, hs.at[5], hr.at[5], prv)
    spread(11, three, [
        (w_in.at[:, pl.ds(c512, HALF)], wh.at[core, pl.ds(cprow, 64)], x_peer(k)) for k in range(1, NX)
    ])

    loads[3].wait()
    loads[8].wait()

    def tap_sum(n, lanes, r0, r1):
        acc = jnp.zeros((r1 - r0, 128), F32)
        for j in range(KW):
            acc = acc + cw_ref[pl.ds(j, 1), lanes] * gf[n, pl.ds(r0 + 11 - j, r1 - r0), :]
        frame = cp * ROWS + r0 + lax.broadcasted_iota(jnp.int32, (r1 - r0, 128), 0)
        at = pl.ds(pl.multiple_of((n % 4) * 128, 128), 128)
        sg[n // 4, r0:r1, at] = jnp.where(frame < length, acc, 0.0).astype(BF)

    def masked_rows(n, lanes, r0, r1):
        frame = cp * ROWS - 8 + r0 + lax.broadcasted_iota(jnp.int32, (r1 - r0, 128), 0)
        ok = (frame >= 0) & (frame < length)
        gf[n, r0:r1] = jnp.where(ok, gext[r0:r1, lanes].astype(F32), 0.0)

    def conv_inside(n, carry):
        lanes = pl.ds(pl.multiple_of(n * 128, 128), 128)
        masked_rows(n, lanes, 8, 200)
        tap_sum(n, lanes, 16, 176)
        return carry

    def conv_edges(n, carry):
        lanes = pl.ds(pl.multiple_of(n * 128, 128), 128)
        masked_rows(n, lanes, 0, 8)
        masked_rows(n, lanes, 200, 208)
        tap_sum(n, lanes, 0, 16)
        tap_sum(n, lanes, 176, 192)
        return carry

    lax.fori_loop(0, 8, conv_inside, 0)

    arrived_if(has_prev, g_lo, hr.at[0], hs.at[0], nxt)
    arrived_if(has_next, g_hi, hr.at[1], hs.at[1], nxt)

    lax.fori_loop(0, 8, conv_edges, 0)
    send(sg.at[1 - core], s2p, gs.at[15], gr.at[15], partner)
    outs = [
        pltpu.make_async_copy(sg.at[0], sg_out.at[0, :, pl.ds(0, HALF)], out_sem.at[0]),
        pltpu.make_async_copy(sg.at[1], sg_out.at[0, :, pl.ds(HALF, HALF)], out_sem.at[1]),
    ]
    outs[0].start()
    outs[1].start()

    arrived_if(cp == 7, vrel, hr.at[8], hs.at[8], across)
    send_if(cp == 7, vrel, v_lo, hs.at[4], hr.at[4], cp_peer(5))
    arrived_if(cp == 0, vrel.at[pl.ds(0, BLK)], hr.at[8], hs.at[8], across)
    send_if(cp == 0, vrel.at[pl.ds(0, BLK)], v_hi, hs.at[5], hr.at[5], cp_peer(3))
    landed(12, o_block)
    spread(13, three, [(o_block, o_block, x_peer(k)) for k in range(1, NX)])

    landed(11, three)

    def whole_block(side, k):
        return wh.at[core, pl.ds(pl.multiple_of((side * NX + (x + NX - k) % NX) * 64, 64), 64)]

    near = [o_block] + [whole_block(yh, k) for k in range(1, NX)]
    for block in near:
        rc(block, block, gs.at[14], gr.at[14], partner).start()

    arrived_if(has_prev, k_lo, hr.at[2], hs.at[2], nxt)
    arrived_if(has_next, k_hi, hr.at[3], hs.at[3], nxt)
    arrived_if(has_prev, v_lo, hr.at[4], hs.at[4], nxt)
    arrived_if(has_next, v_hi, hr.at[5], hs.at[5], nxt)

    def edge_fwd(t, carry):
        forward_tile(3 * t)
        return carry

    lax.fori_loop(0, 2, edge_fwd, 0)
    send(a_own, a_par, gs.at[16], gr.at[16], partner)

    arrived(s2p, gr.at[15], gs.at[15], partner)
    arrived(a_par, gr.at[16], gs.at[16], partner)

    low, high = pl.ds(0, 64), pl.ds(64, 64)
    far = (x + 2) % NX
    for w in range(2):
        cs = slice(w * 256, w * 256 + 256)
        dw = dot(a_own[...], sg[core, :, cs], CONTRACT_FIRST)
        dw = dw + dot(a_par[...], s2p[:, cs], CONTRACT_FIRST)
        dw = dw.astype(BF)
        per = 256 // CW
        for u in range(per):
            c = w * per + u
            us = slice(u * CW, u * CW + CW)
            for xt in range(NX):
                xs[c, xt, 0:64] = dw[64 * xt:64 * xt + 64, us]
                xs[c, xt, 64:128] = dw[256 + 64 * xt:256 + 64 * xt + 64, us]
            send(xs.at[c, far, low], xrel.at[c, 0], xss.at[c, 0], xrs.at[c, 0], x_peer(1))
            send(xs.at[c, far, high], xrel.at[c, 1], xss.at[c, 1], xrs.at[c, 1], x_peer(3))
        for u in range(per):
            c = w * per + u
            send(xs.at[c, (x + 1) % NX, high], xr.at[c, 0, high], xss.at[c, 2], xrs.at[c, 2], x_peer(1))
            send(xs.at[c, (x + 3) % NX, low], xr.at[c, 1, low], xss.at[c, 3], xrs.at[c, 3], x_peer(3))

    landed(13, three)
    spread(14, wh.at[core, pl.ds(0, 448)], [
        (whole_block(1 - yh, k), whole_block(1 - yh, k), partner) for k in range(1, NX)
    ])

    for c in range(NC):
        arrived(xrel.at[c, 0], xrs.at[c, 0], xss.at[c, 0], partner)
        xc[c, 0] = (xs[c, (x + 1) % NX, 0:64].astype(F32) + xrel[c, 0].astype(F32)).astype(BF)
        send(xc.at[c, 0], xr.at[c, 0, low], xss.at[c, 4], xrs.at[c, 4], x_peer(1))
        arrived(xrel.at[c, 1], xrs.at[c, 1], xss.at[c, 1], partner)
        xc[c, 1] = (xs[c, (x + 3) % NX, 64:128].astype(F32) + xrel[c, 1].astype(F32)).astype(BF)
        send(xc.at[c, 1], xr.at[c, 1, high], xss.at[c, 5], xrs.at[c, 5], x_peer(3))

    loads[4].wait()
    loads[5].wait()
    loads[6].wait()
    landed(14, wh.at[1 - core, pl.ds(0, 448)])

    t_frame = cp * ROWS + lax.broadcasted_iota(jnp.int32, (ROWS, 128), 0)
    t_valid = (t_frame < length).astype(F32)

    def tap_chunk(m, carry):
        at = pl.ds(pl.multiple_of((m % 2) * 256, 256), 256)
        proj = dot(a_own[...], wh[m // 2, :, at], PLAIN)
        for u in range(2):
            n = 2 * m + u
            lanes = pl.ds(pl.multiple_of(n * 128, 128), 128)
            mixed = (sbuf[:, lanes].astype(F32) + proj[:, 128 * u:128 * u + 128]) * t_valid
            rows = [
                jnp.sum(mixed * gf[n, pl.ds(11 - j, ROWS), :], axis=0, keepdims=True)
                for j in range(KW)
            ]
            rows.append(jnp.zeros((1, 128), F32))
            cpart[n] = jnp.concatenate(rows, axis=0)
        return carry

    lax.fori_loop(0, 4, tap_chunk, 0)
    taps = [(cpart.at[4 * (1 - core) + x], cxr.at[4], partner)]
    for k in range(1, NX):
        to_x = (x + k) % NX
        taps.append((cpart.at[4 * core + to_x], cxr.at[k], x_peer(k)))
        taps.append((cpart.at[4 * (1 - core) + to_x], cxr.at[4 + k], x_peer(k, 1 - core)))
    spread(4, cpart.at[pl.ds(0, 7)], taps)

    def x_sum(c):
        arrived(xr.at[c, 0, high], xrs.at[c, 2], xss.at[c, 2], partner)
        arrived(xr.at[c, 1, low], xrs.at[c, 3], xss.at[c, 3], partner)
        arrived(xr.at[c, 0, low], xrs.at[c, 4], xss.at[c, 4], partner)
        arrived(xr.at[c, 1, high], xrs.at[c, 5], xss.at[c, 5], partner)
        total = xs[c, x].astype(F32) + xr[c, 0].astype(F32) + xr[c, 1].astype(F32)
        return total

    ys[...] = x_sum(0).astype(BF).reshape(NY, 16, CW)
    spread(0, ys.at[pl.ds(0, 7)], [(ys.at[(y + k) % NY], yr.at[k], y_peer(k)) for k in FAR])
    total = x_sum(1)
    for t in range(NZ):
        for h in range(2):
            bs[t, h] = total[64 * h + 8 * t:64 * h + 8 * t + 8].astype(BF)
    spread(1, bs.at[pl.ds(0, 7)], [(bs.at[(z + k) % NZ], br.at[k], z_peer(k)) for k in FAR])

    grad_att = dot(sg[0], wh[0], CONTRACT_LAST) + dot(sg[1], wh[1], CONTRACT_LAST)
    ag[...] = grad_att.astype(BF)
    kgacc[...] = jnp.zeros((EXT, HD), F32)
    vgacc[...] = jnp.zeros((EXT, HD), F32)

    def backward_tile(i):
        r0 = pl.multiple_of(i * QT, 16)
        for g in range(2):
            cols = slice(256 * g, 256 * g + 256)
            kk = kext[pl.ds(r0, KT), cols]
            vv = vext[pl.ds(r0, KT), cols]
            qs = stacked(qbuf[pl.ds(r0, QT), cols])
            gs = stacked(ag[pl.ds(r0, QT), cols])
            p = psave[i, g]
            dprob = dot(gs, vv, CONTRACT_LAST)
            inner = jnp.sum(p * dprob, axis=1, keepdims=True)
            ds = (p * (dprob - inner)).astype(BF)
            qg_v[pl.ds(r0, QT), cols] = (unstacked(dot(ds, kk, PLAIN)) * SCALE).astype(BF)
            at = pl.ds(r0, KT)
            kgacc[at, cols] = kgacc[at, cols] + dot(ds, qs, CONTRACT_FIRST)
            vgacc[at, cols] = vgacc[at, cols] + dot(p.astype(BF), gs, CONTRACT_FIRST)

    def edge_bwd(t, carry):
        backward_tile(3 * t)
        return carry

    lax.fori_loop(0, 2, edge_bwd, 0)
    to_prev[0] = (kgacc[0:48] * SCALE).astype(BF)
    to_prev[1] = vgacc[0:48].astype(BF)
    to_next[0] = (kgacc[240:264] * SCALE).astype(BF)
    to_next[1] = vgacc[240:264].astype(BF)

    send_if(cp == 3, to_next.at[1], rel_next, hs.at[9], hr.at[9], across)
    send_if(cp == 4, to_prev.at[1], rel_prev, hs.at[9], hr.at[9], across)
    send_if(has_prev, to_prev.at[0], from_next.at[0], hs.at[6], hr.at[6], prv)
    send_if(has_next, to_next.at[0], from_prev.at[0], hs.at[7], hr.at[7], nxt)
    send_if(has_prev & (cp != 4), to_prev.at[1], from_next.at[1], hs.at[10], hr.at[10], prv)
    send_if(has_next & (cp != 3), to_next.at[1], from_prev.at[1], hs.at[11], hr.at[11], nxt)

    total = cpart[4 * core + x]
    landed(4, cxr.at[pl.ds(1, 7)])
    for k in range(1, 8):
        total = total + cxr[k]
    cz[z] = total
    spread(5, cz.at[pl.ds(0, 7)], [(cz.at[z], cz.at[z], z_peer(k)) for k in FAR])

    def inner_bwd(t, carry):
        backward_tile(1 + t)
        return carry

    lax.fori_loop(0, 2, inner_bwd, 0)
    outs.append(pltpu.make_async_copy(qg_v, qg_out.at[0], out_sem.at[2]))
    outs[-1].start()

    total = ys[y].astype(F32)
    landed(0, yr.at[pl.ds(1, 7)])
    for k in range(1, NY):
        total = total + yr[k].astype(F32)
    zr[z] = total.astype(BF)
    spread(2, zr.at[pl.ds(0, 7)], [(zr.at[z], zr.at[z], z_peer(k)) for k in FAR])
    total = bs[z].astype(F32)
    landed(1, br.at[pl.ds(1, 7)])
    for k in range(1, NZ):
        total = total + br[k].astype(F32)
    bsum[...] = total.astype(BF)
    bz[y] = bsum[yh]
    spread(3, bz.at[pl.ds(0, 7)], [(bsum.at[((y + k) % NY) // NYL], bz.at[y], y_peer(k)) for k in FAR])

    landed(5, cz.at[pl.ds(0, 7)])
    total = cz[0]
    for t in range(1, NZ):
        total = total + cz[t]
    cy[y] = total
    spread(6, cy.at[pl.ds(0, 7)], [(cy.at[y], cy.at[y], y_peer(k)) for k in FAR])

    landed(2, zr.at[pl.ds(0, 7)])
    total = zr[0].astype(F32)
    for t in range(1, NZ):
        total = total + zr[t].astype(F32)
    fin[4 * core + yl] = total.astype(BF)
    mine = fin.at[4 * core + yl]
    others = [(mine, mine, partner)]
    for k in (2, 1, 3):
        others += [(mine, mine, yl_peer(k)), (mine, mine, yl_peer(k, 1 - core))]
    spread(8, fin.at[pl.ds(0, 7)], others)
    landed(3, bz.at[pl.ds(0, 7)])
    total = bz[0].astype(F32)
    for t in range(1, NY):
        total = total + bz[t].astype(F32)
    finb[core, z] = total.astype(BF)
    mine = finb.at[core, z]
    spread(9, finb.at[core, pl.ds(0, 7)], [(mine, mine, z_peer(k)) for k in FAR])

    arrived_if(cp == 7, rel_next, hr.at[9], hs.at[9], across)
    send_if(cp == 7, rel_next, from_prev.at[1], hs.at[11], hr.at[11], cp_peer(5))
    arrived_if(cp == 0, rel_prev, hr.at[9], hs.at[9], across)
    send_if(cp == 0, rel_prev, from_next.at[1], hs.at[10], hr.at[10], cp_peer(3))

    landed(6, cy.at[pl.ds(0, 7)])
    total = cy[0]
    for t in range(1, NY):
        total = total + cy[t]
    cx[4 * core + x] = total
    mine = cx.at[4 * core + x]
    others = [(mine, mine, partner)]
    for k in range(1, NX):
        others += [(mine, mine, x_peer(k)), (mine, mine, x_peer(k, 1 - core))]
    spread(7, cx.at[pl.ds(0, 7)], others)

    landed(9, finb.at[core, pl.ds(0, 7)])
    spread(10, finb.at[core], [(finb.at[core], finb.at[core], partner)])

    arrived_if(has_next, from_next.at[0], hr.at[6], hs.at[6], prv)
    arrived_if(has_prev, from_prev.at[0], hr.at[7], hs.at[7], prv)
    arrived_if(has_next, from_next.at[1], hr.at[10], hs.at[10], prv)
    arrived_if(has_prev, from_prev.at[1], hr.at[11], hs.at[11], prv)
    for src, acc, dst, scale in ((0, kgacc, kg_v, SCALE), (1, vgacc, vg_v, 1.0)):
        low_rows = acc[48:80] * scale
        extra = from_prev[src].astype(F32)
        dst[0:32] = jnp.concatenate([low_rows[0:BLK] + extra, low_rows[BLK:32]], axis=0).astype(BF)
        dst[32:144] = (acc[80:192] * scale).astype(BF)
        dst[144:192] = (acc[192:240] * scale + from_next[src].astype(F32)).astype(BF)
    outs.append(pltpu.make_async_copy(kg_v, kg_out.at[0], out_sem.at[3]))
    outs[-1].start()
    outs.append(pltpu.make_async_copy(vg_v, vg_out.at[0], out_sem.at[4]))
    outs[-1].start()

    landed(7, cx.at[pl.ds(0, 7)])
    for h in range(2):
        for b in range(NX):
            at = h * HALF + b * 128
            cg_v[:, at:at + 128] = cx[4 * h + b, 0:KW]
    outs.append(pltpu.make_async_copy(cg_v, cg_out, out_sem.at[6]))
    outs[-1].start()

    landed(8, fin.at[pl.ds(0, 7)])
    for h in range(2):
        for t in range(NYL):
            wg_v[16 * t:16 * t + 16, h * HALF:h * HALF + CW] = fin[4 * h + t].astype(F32)
    landed(10, finb.at[1 - core])
    for h in range(2):
        for t in range(NZ):
            wg_v[8 * t:8 * t + 8, h * HALF + CW:h * HALF + HALF] = finb[h, t].astype(F32)
    outs.append(pltpu.make_async_copy(wg_v, wg_out, out_sem.at[5]))
    outs[-1].start()

    for c in sent:
        c.wait_send()
    for cond, c in sent_if:
        pl.when(cond)(c.wait_send)
    for c in outs:
        c.wait()


def finish(*refs):
    ins, outs, sem = refs[:6], refs[6:12], refs[12]
    copies = [pltpu.make_async_copy(a, b, sem.at[n]) for n, (a, b) in enumerate(zip(ins, outs))]
    for c in copies:
        c.start()
    for c in copies:
        c.wait()


def body(
    queries, key_rows, value_rows, stream_in, out_grad, out_weight, conv_weight, lengths, offsets
):
    hbm = pl.BlockSpec(memory_space=pltpu.HBM)
    free = pl.BlockSpec(memory_space=pl.ANY)
    dma = pltpu.SemaphoreType.DMA
    sds = jax.ShapeDtypeStruct
    V = pltpu.VMEM
    held = lambda a: pltpu.with_memory_space_constraint(a, pltpu.HBM)
    shapes = [
            sds((1, ROWS, HD), BF), sds((1, ROWS, HD), BF), sds((1, ROWS, HD), BF),
            sds((1, ROWS, D), BF), sds((64, D), F32), sds((KW, D), F32),
        ]
    made = pl.pallas_call(
        kernel,
        in_specs=[pl.BlockSpec(memory_space=pltpu.SMEM)] + [hbm] * 8,
        out_specs=[free] * 6,
        out_shape=shapes,
        scratch_shapes=[
            pltpu.SMEM((1, 2), jnp.int32), V((KW, D), F32),
            V((EXT, HD), BF), V((EXT, HD), BF), V((48, HD), BF), V((ROWS, HD), BF), V((ROWS, D), BF),
            V((GEXT, D), BF), V((8, GEXT, 128), F32), V((2, HD, HALF), BF),
            V((ROWS, HD), BF), V((ROWS, HD), BF), V((2, ROWS, HALF), BF), V((ROWS, HALF), BF),
            V((ROWS, HD), BF), V((4, 2, 4 * QT, KT), F32),
            V((EXT, HD), F32), V((EXT, HD), F32),
            V((2, 48, HD), BF), V((2, BLK, HD), BF), V((2, 48, HD), BF), V((2, BLK, HD), BF),
            V((48, HD), BF), V((BLK, HD), BF),
            V((ROWS, HD), BF), V((ROWS, HD), BF), V((ROWS, HD), BF), V((64, D), F32), V((KW, D), F32),
            V((NC, NX, 128, CW), BF), V((NC, 2, 128, CW), BF), V((NC, 2, 64, CW), BF), V((NC, 2, 64, CW), BF),
            V((NY, 16, CW), BF), V((NY, 16, CW), BF), V((NZ, 16, CW), BF), V((8, 16, CW), BF),
            V((NZ, 2, 8, CW), BF), V((NZ, 2, 8, CW), BF), V((2, 8, CW), BF), V((NY, 8, CW), BF),
            V((2, NZ, 8, CW), BF),
            V((8, 8, 128), F32), V((8, 8, 128), F32),
            V((NY, 8, 128), F32), V((NZ, 8, 128), F32), V((8, 8, 128), F32),
            dma((9,)), dma((7,)), dma((12,)), dma((12,)), dma((NC, 6)), dma((NC, 6)), dma((17,)), dma((17,)),
        ],
        compiler_params=pltpu.CompilerParams(
            collective_id=0, has_side_effects=True, vmem_limit_bytes=48 * 1024 * 1024
        ),
        name="fused_backward",
    )(lengths, *map(held, (
        offsets, queries, key_rows, value_rows, stream_in, out_grad, out_weight, conv_weight
    )))
    return pl.pallas_call(
        finish,
        in_specs=[free] * 6,
        out_specs=[free] * 6,
        out_shape=shapes,
        scratch_shapes=[dma((6,))],
        compiler_params=pltpu.CompilerParams(vmem_limit_bytes=1024 * 1024),
        name="finish",
    )(*made)


def solution(mesh):
    row = P("dp", "cp", None)
    return jax.shard_map(
        body,
        mesh=mesh,
        in_specs=(row, row, row, row, row, P("cp", None), P(), P("dp"), P("dp", None)),
        out_specs=(row, row, row, row, P("cp", None), P()),
        check_vma=False,
    )
```

```python
import jax
import jax.numpy as jnp
from jax import lax
from jax.experimental import pallas as pl
from jax.experimental.pallas import tpu as pltpu
from jax.sharding import PartitionSpec as P

HSZ = 64
BLK = 24
KW = 7
ROWS = 192
HD = 512
D = 1024
HALF = 512
NX, NY, NYL, NZ = 4, 8, 4, 8
NC = 2
CW = HALF // NC
QT = 48
KT = 128
EXT = 272
GEXT = 208
NEG = -1e30
SCALE = HSZ ** -0.5
BF = jnp.bfloat16
F32 = jnp.float32
MESH = pl.DeviceIdType.MESH
FAR = (4, 3, 5, 2, 6, 1, 7)

CONTRACT_LAST = (((1,), (1,)), ((), ()))
CONTRACT_FIRST = (((0,), (0,)), ((), ()))
PLAIN = (((1,), (0,)), ((), ()))


def dot(a, b, dims):
    return lax.dot_general(a, b, dims, preferred_element_type=F32)


def kernel(
    len_ref, off_in, q_in, k_in, v_in, s_in, g_in, w_in, cw_in,
    qg_out, kg_out, vg_out, sg_out, wg_out, cg_out,
    off_ref, cw_ref, kext, vext, vrel, qbuf, sbuf, gext, gf, wh, a_own, a_par, sg, s2p, ag, psave,
    kgacc, vgacc, to_prev, to_next, from_next, from_prev, rel_prev, rel_next,
    qg_v, kg_v, vg_v, wg_v, cg_v,
    xs, xr, xc, xrel, ys, yr, zr, fin, bs, br, bsum, bz, finb,
    cpart, cxr, cy, cz, cx,
    loc, out_sem, hs, hr, xss, xrs, gs, gr,
):
    cp = lax.axis_index("cp")
    dp = lax.axis_index("dp")
    yh = cp // NX
    x = cp % NX
    core = dp % 2
    z = (dp // 2) % NZ
    yl = dp // (2 * NZ)
    y = yh * NYL + yl

    def dev(y_to, x_to, z_to, core_to):
        return {
            "cp": (y_to // NYL) * NX + x_to,
            "dp": ((y_to % NYL) * NZ + z_to) * 2 + core_to,
        }

    def x_peer(k, to_core=None):
        return dev(y, (x + k) % NX, z, core if to_core is None else to_core)

    def y_peer(k):
        return dev((y + k) % NY, x, z, core)

    def z_peer(k):
        return dev(y, x, (z + k) % NZ, core)

    def yl_peer(k, to_core=None):
        return dev(yh * NYL + (yl + k) % NYL, x, z, core if to_core is None else to_core)

    partner = dev(y, x, z, 1 - core)

    def cp_peer(k):
        return {"cp": (cp + k) % 8, "dp": dp}

    nxt, prv, across = cp_peer(1), cp_peer(7), cp_peer(4)

    def rc(src, dst, ssem, rsem, to):
        return pltpu.make_async_remote_copy(
            src_ref=src, dst_ref=dst, send_sem=ssem, recv_sem=rsem,
            device_id=to, device_id_type=MESH,
        )

    sent = []
    sent_if = []

    def send(src, dst, ssem, rsem, to):
        c = rc(src, dst, ssem, rsem, to)
        c.start()
        sent.append(c)

    def send_if(cond, src, dst, ssem, rsem, to):
        c = rc(src, dst, ssem, rsem, to)
        pl.when(cond)(c.start)
        sent_if.append((cond, c))

    def spread(n, whole, copies):
        for src, dst, to in copies:
            rc(src, dst, gs.at[n], gr.at[n], to).start()
        sent.append(rc(whole, whole, gs.at[n], gr.at[n], partner))

    def landed(n, whole):
        rc(whole, whole, gs.at[n], gr.at[n], partner).wait_recv()

    def arrived(dst, rsem, ssem, to):
        rc(dst, dst, ssem, rsem, to).wait_recv()

    def arrived_if(cond, dst, rsem, ssem, to):
        pl.when(cond)(rc(dst, dst, ssem, rsem, to).wait_recv)

    barrier = pltpu.get_barrier_semaphore()
    greet = [y_peer(k) for k in (4, 3, 5, 2, 6, 1, 7)]
    greet += [z_peer(k) for k in (4, 3, 5, 2, 6, 1, 7)]
    greet += [nxt, prv] + [x_peer(k) for k in (2, 1, 3)] + [partner]
    greet += [yl_peer(k, 1 - core) for k in (2, 1, 3)] + [x_peer(k, 1 - core) for k in (2, 1, 3)] + [cp_peer(3), cp_peer(5)]
    for to in greet:
        pl.semaphore_signal(barrier, inc=1, device_id=to, device_id_type=MESH)

    c512 = pl.multiple_of(core * HALF, HALF)
    cprow = pl.multiple_of(cp * 64, 64)
    orow = pl.multiple_of(((cp + 4) % 8) * 64, 64)
    ylrow = pl.multiple_of(yl * 16, 16)
    wq_mine = pl.multiple_of(cp * 64 + yl * 16, 16)

    loads = [
        pltpu.make_async_copy(k_in.at[0], kext.at[pl.ds(48, ROWS)], loc.at[0]),
        pltpu.make_async_copy(q_in.at[0], qbuf, loc.at[1]),
        pltpu.make_async_copy(v_in.at[0], vext.at[pl.ds(48, ROWS)], loc.at[2]),
        pltpu.make_async_copy(g_in.at[0], gext.at[pl.ds(8, ROWS)], loc.at[3]),
        pltpu.make_async_copy(w_in.at[:, pl.ds(0, HALF)], wh.at[0, pl.ds(cprow, 64)], loc.at[4]),
        pltpu.make_async_copy(w_in.at[:, pl.ds(HALF, HALF)], wh.at[1, pl.ds(cprow, 64)], loc.at[5]),
        pltpu.make_async_copy(s_in.at[0], sbuf, loc.at[6]),
        pltpu.make_async_copy(off_in, off_ref, loc.at[7]),
        pltpu.make_async_copy(cw_in, cw_ref, loc.at[8]),
    ]
    for n in (7, 0, 1, 2, 3, 8, 4, 5, 6):
        loads[n].start()

    has_prev = cp > 0
    has_next = cp < 7
    kext[264:272] = jnp.zeros((8, HD), BF)
    vext[264:272] = jnp.zeros((8, HD), BF)
    to_clear = jnp.zeros((48, HD), BF)

    @pl.when(cp == 0)
    def _():
        kext[0:48] = to_clear
        vext[0:48] = to_clear
        gext[0:8] = jnp.zeros((8, D), BF)
        from_prev[...] = jnp.zeros((2, BLK, HD), BF)

    @pl.when(cp == 7)
    def _():
        kext[240:264] = to_clear[0:BLK]
        vext[240:264] = to_clear[0:BLK]
        gext[200:208] = jnp.zeros((8, D), BF)
        from_next[...] = jnp.zeros((2, 48, HD), BF)

    loads[7].wait()
    length = len_ref[0]
    back = off_ref[0, 0]
    ahead = off_ref[0, 1]
    lane = lax.broadcasted_iota(jnp.int32, (1, 256), 1)
    head_f = [((lane // HSZ) == h).astype(F32) for h in range(4)]
    head_b = [m.astype(BF) for m in head_f]
    row_i = lax.broadcasted_iota(jnp.int32, (4 * QT, KT), 0)
    col_i = lax.broadcasted_iota(jnp.int32, (4 * QT, KT), 1)
    rel = col_i // BLK - 2 - (row_i % QT) // BLK
    reach = (rel >= -back) & (rel <= ahead)

    def stacked(block):
        return jnp.concatenate([block * head_b[h] for h in range(4)], axis=0)

    def unstacked(block):
        total = block[0:QT] * head_f[0]
        for h in range(1, 4):
            total = total + block[h * QT:(h + 1) * QT] * head_f[h]
        return total

    def forward_tile(i):
        r0 = pl.multiple_of(i * QT, 16)
        key_frame = cp * ROWS + i * QT - 2 * BLK + col_i
        ok = reach & (key_frame >= 0) & (key_frame < length)
        frame = cp * ROWS + i * QT + lax.broadcasted_iota(jnp.int32, (QT, 1), 0)
        valid = (frame < length).astype(F32)
        for g in range(2):
            cols = slice(256 * g, 256 * g + 256)
            kk = kext[pl.ds(r0, KT), cols]
            vv = vext[pl.ds(r0, KT), cols]
            qs = stacked(qbuf[pl.ds(r0, QT), cols])
            s = jnp.where(ok, dot(qs, kk, CONTRACT_LAST) * SCALE, NEG)
            e = jnp.exp(s - jnp.max(s, axis=1, keepdims=True))
            p = e / jnp.sum(e, axis=1, keepdims=True)
            psave[i, g] = p
            o = unstacked(dot(p.astype(BF), vv, PLAIN))
            a_own[pl.ds(r0, QT), cols] = (o * valid).astype(BF)

    for n in (0, 1, 2):
        loads[n].wait()

    def inner_fwd(t, carry):
        forward_tile(1 + t)
        return carry

    lax.fori_loop(0, 2, inner_fwd, 0)

    pl.semaphore_wait(barrier, len(greet))

    gi, ki, vi = g_in.at[0], k_in.at[0], v_in.at[0]
    k_lo, k_hi = kext.at[pl.ds(0, 48)], kext.at[pl.ds(240, BLK)]
    v_lo, v_hi = vext.at[pl.ds(0, 48)], vext.at[pl.ds(240, BLK)]
    g_lo, g_hi = gext.at[pl.ds(0, 8)], gext.at[pl.ds(200, 8)]
    send_if(has_next, gi.at[pl.ds(184, 8)], g_lo, hs.at[0], hr.at[0], nxt)
    send_if(has_prev, gi.at[pl.ds(0, 8)], g_hi, hs.at[1], hr.at[1], prv)
    wq = wh.at[core, pl.ds(wq_mine, 16)]
    o_block = wh.at[core, pl.ds(orow, 64)]
    three = wh.at[core, pl.ds(0, 192)]
    spread(12, o_block, [
        (w_in.at[pl.ds(ylrow, 16), pl.ds(c512, HALF)], wq, dev((1 - yh) * NYL + k, x, z, core))
        for k in range(NYL)
    ])
    v_last, v_first = vi.at[pl.ds(144, 48)], vi.at[pl.ds(0, BLK)]
    send_if(cp == 3, v_last, vrel, hs.at[8], hr.at[8], across)
    send_if(cp == 4, v_first, vrel.at[pl.ds(0, BLK)], hs.at[8], hr.at[8], across)
    send_if(has_next, ki.at[pl.ds(144, 48)], k_lo, hs.at[2], hr.at[2], nxt)
    send_if(has_prev, ki.at[pl.ds(0, BLK)], k_hi, hs.at[3], hr.at[3], prv)
    send_if(has_next & (cp != 3), v_last, v_lo, hs.at[4], hr.at[4], nxt)
    send_if(has_prev & (cp != 4), v_first, v_hi, hs.at[5], hr.at[5], prv)
    spread(11, three, [
        (w_in.at[:, pl.ds(c512, HALF)], wh.at[core, pl.ds(cprow, 64)], x_peer(k)) for k in range(1, NX)
    ])

    loads[3].wait()
    loads[8].wait()

    def tap_sum(n, lanes, r0, r1):
        acc = jnp.zeros((r1 - r0, 128), F32)
        for j in range(KW):
            acc = acc + cw_ref[pl.ds(j, 1), lanes] * gf[n, pl.ds(r0 + 11 - j, r1 - r0), :]
        frame = cp * ROWS + r0 + lax.broadcasted_iota(jnp.int32, (r1 - r0, 128), 0)
        at = pl.ds(pl.multiple_of((n % 4) * 128, 128), 128)
        sg[n // 4, r0:r1, at] = jnp.where(frame < length, acc, 0.0).astype(BF)

    def masked_rows(n, lanes, r0, r1):
        frame = cp * ROWS - 8 + r0 + lax.broadcasted_iota(jnp.int32, (r1 - r0, 128), 0)
        ok = (frame >= 0) & (frame < length)
        gf[n, r0:r1] = jnp.where(ok, gext[r0:r1, lanes].astype(F32), 0.0)

    def conv_inside(n, carry):
        lanes = pl.ds(pl.multiple_of(n * 128, 128), 128)
        masked_rows(n, lanes, 8, 200)
        tap_sum(n, lanes, 16, 176)
        return carry

    def conv_edges(n, carry):
        lanes = pl.ds(pl.multiple_of(n * 128, 128), 128)
        masked_rows(n, lanes, 0, 8)
        masked_rows(n, lanes, 200, 208)
        tap_sum(n, lanes, 0, 16)
        tap_sum(n, lanes, 176, 192)
        return carry

    lax.fori_loop(0, 8, conv_inside, 0)

    arrived_if(has_prev, g_lo, hr.at[0], hs.at[0], nxt)
    arrived_if(has_next, g_hi, hr.at[1], hs.at[1], nxt)

    lax.fori_loop(0, 8, conv_edges, 0)
    send(sg.at[1 - core], s2p, gs.at[15], gr.at[15], partner)
    outs = [
        pltpu.make_async_copy(sg.at[0], sg_out.at[0, :, pl.ds(0, HALF)], out_sem.at[0]),
        pltpu.make_async_copy(sg.at[1], sg_out.at[0, :, pl.ds(HALF, HALF)], out_sem.at[1]),
    ]
    outs[0].start()
    outs[1].start()

    arrived_if(cp == 7, vrel, hr.at[8], hs.at[8], across)
    send_if(cp == 7, vrel, v_lo, hs.at[4], hr.at[4], cp_peer(5))
    arrived_if(cp == 0, vrel.at[pl.ds(0, BLK)], hr.at[8], hs.at[8], across)
    send_if(cp == 0, vrel.at[pl.ds(0, BLK)], v_hi, hs.at[5], hr.at[5], cp_peer(3))
    landed(12, o_block)
    spread(13, three, [(o_block, o_block, x_peer(k)) for k in range(1, NX)])

    arrived_if(has_prev, k_lo, hr.at[2], hs.at[2], nxt)
    arrived_if(has_next, k_hi, hr.at[3], hs.at[3], nxt)
    arrived_if(has_prev, v_lo, hr.at[4], hs.at[4], nxt)
    arrived_if(has_next, v_hi, hr.at[5], hs.at[5], nxt)

    def edge_fwd(t, carry):
        forward_tile(3 * t)
        return carry

    lax.fori_loop(0, 2, edge_fwd, 0)
    send(a_own, a_par, gs.at[16], gr.at[16], partner)

    landed(11, three)

    def whole_block(side, k):
        return wh.at[core, pl.ds(pl.multiple_of((side * NX + (x + NX - k) % NX) * 64, 64), 64)]

    near = [o_block] + [whole_block(yh, k) for k in range(1, NX)]
    for block in near:
        rc(block, block, gs.at[14], gr.at[14], partner).start()

    arrived(s2p, gr.at[15], gs.at[15], partner)
    arrived(a_par, gr.at[16], gs.at[16], partner)

    low, high = pl.ds(0, 64), pl.ds(64, 64)
    far = (x + 2) % NX
    for w in range(2):
        cs = slice(w * 256, w * 256 + 256)
        dw = dot(a_own[...], sg[core, :, cs], CONTRACT_FIRST)
        dw = dw + dot(a_par[...], s2p[:, cs], CONTRACT_FIRST)
        dw = dw.astype(BF)
        per = 256 // CW
        for u in range(per):
            c = w * per + u
            us = slice(u * CW, u * CW + CW)
            for xt in range(NX):
                xs[c, xt, 0:64] = dw[64 * xt:64 * xt + 64, us]
                xs[c, xt, 64:128] = dw[256 + 64 * xt:256 + 64 * xt + 64, us]
            send(xs.at[c, far, low], xrel.at[c, 0], xss.at[c, 0], xrs.at[c, 0], x_peer(1))
            send(xs.at[c, far, high], xrel.at[c, 1], xss.at[c, 1], xrs.at[c, 1], x_peer(3))
        for u in range(per):
            c = w * per + u
            send(xs.at[c, (x + 1) % NX, high], xr.at[c, 0, high], xss.at[c, 2], xrs.at[c, 2], x_peer(1))
            send(xs.at[c, (x + 3) % NX, low], xr.at[c, 1, low], xss.at[c, 3], xrs.at[c, 3], x_peer(3))

    landed(13, three)
    spread(14, wh.at[core, pl.ds(0, 448)], [
        (whole_block(1 - yh, k), whole_block(1 - yh, k), partner) for k in range(1, NX)
    ])

    for c in range(NC):
        arrived(xrel.at[c, 0], xrs.at[c, 0], xss.at[c, 0], partner)
        xc[c, 0] = (xs[c, (x + 1) % NX, 0:64].astype(F32) + xrel[c, 0].astype(F32)).astype(BF)
        send(xc.at[c, 0], xr.at[c, 0, low], xss.at[c, 4], xrs.at[c, 4], x_peer(1))
        arrived(xrel.at[c, 1], xrs.at[c, 1], xss.at[c, 1], partner)
        xc[c, 1] = (xs[c, (x + 3) % NX, 64:128].astype(F32) + xrel[c, 1].astype(F32)).astype(BF)
        send(xc.at[c, 1], xr.at[c, 1, high], xss.at[c, 5], xrs.at[c, 5], x_peer(3))

    loads[4].wait()
    loads[5].wait()
    loads[6].wait()
    landed(14, wh.at[1 - core, pl.ds(0, 448)])

    t_frame = cp * ROWS + lax.broadcasted_iota(jnp.int32, (ROWS, 128), 0)
    t_valid = (t_frame < length).astype(F32)

    def tap_chunk(m, carry):
        at = pl.ds(pl.multiple_of((m % 2) * 256, 256), 256)
        proj = dot(a_own[...], wh[m // 2, :, at], PLAIN)
        for u in range(2):
            n = 2 * m + u
            lanes = pl.ds(pl.multiple_of(n * 128, 128), 128)
            mixed = (sbuf[:, lanes].astype(F32) + proj[:, 128 * u:128 * u + 128]) * t_valid
            rows = [
                jnp.sum(mixed * gf[n, pl.ds(11 - j, ROWS), :], axis=0, keepdims=True)
                for j in range(KW)
            ]
            rows.append(jnp.zeros((1, 128), F32))
            cpart[n] = jnp.concatenate(rows, axis=0)
        return carry

    lax.fori_loop(0, 4, tap_chunk, 0)
    taps = [(cpart.at[4 * (1 - core) + x], cxr.at[4], partner)]
    for k in range(1, NX):
        to_x = (x + k) % NX
        taps.append((cpart.at[4 * core + to_x], cxr.at[k], x_peer(k)))
        taps.append((cpart.at[4 * (1 - core) + to_x], cxr.at[4 + k], x_peer(k, 1 - core)))
    spread(4, cpart.at[pl.ds(0, 7)], taps)

    def x_sum(c):
        arrived(xr.at[c, 0, high], xrs.at[c, 2], xss.at[c, 2], partner)
        arrived(xr.at[c, 1, low], xrs.at[c, 3], xss.at[c, 3], partner)
        arrived(xr.at[c, 0, low], xrs.at[c, 4], xss.at[c, 4], partner)
        arrived(xr.at[c, 1, high], xrs.at[c, 5], xss.at[c, 5], partner)
        total = xs[c, x].astype(F32) + xr[c, 0].astype(F32) + xr[c, 1].astype(F32)
        return total

    ys[...] = x_sum(0).astype(BF).reshape(NY, 16, CW)
    spread(0, ys.at[pl.ds(0, 7)], [(ys.at[(y + k) % NY], yr.at[k], y_peer(k)) for k in FAR])
    total = x_sum(1)
    for t in range(NZ):
        for h in range(2):
            bs[t, h] = total[64 * h + 8 * t:64 * h + 8 * t + 8].astype(BF)
    spread(1, bs.at[pl.ds(0, 7)], [(bs.at[(z + k) % NZ], br.at[k], z_peer(k)) for k in FAR])

    grad_att = dot(sg[0], wh[0], CONTRACT_LAST) + dot(sg[1], wh[1], CONTRACT_LAST)
    ag[...] = grad_att.astype(BF)
    kgacc[...] = jnp.zeros((EXT, HD), F32)
    vgacc[...] = jnp.zeros((EXT, HD), F32)

    def backward_tile(i):
        r0 = pl.multiple_of(i * QT, 16)
        for g in range(2):
            cols = slice(256 * g, 256 * g + 256)
            kk = kext[pl.ds(r0, KT), cols]
            vv = vext[pl.ds(r0, KT), cols]
            qs = stacked(qbuf[pl.ds(r0, QT), cols])
            gs = stacked(ag[pl.ds(r0, QT), cols])
            p = psave[i, g]
            dprob = dot(gs, vv, CONTRACT_LAST)
            inner = jnp.sum(p * dprob, axis=1, keepdims=True)
            ds = (p * (dprob - inner)).astype(BF)
            qg_v[pl.ds(r0, QT), cols] = (unstacked(dot(ds, kk, PLAIN)) * SCALE).astype(BF)
            at = pl.ds(r0, KT)
            kgacc[at, cols] = kgacc[at, cols] + dot(ds, qs, CONTRACT_FIRST)
            vgacc[at, cols] = vgacc[at, cols] + dot(p.astype(BF), gs, CONTRACT_FIRST)

    def edge_bwd(t, carry):
        backward_tile(3 * t)
        return carry

    lax.fori_loop(0, 2, edge_bwd, 0)
    to_prev[0] = (kgacc[0:48] * SCALE).astype(BF)
    to_prev[1] = vgacc[0:48].astype(BF)
    to_next[0] = (kgacc[240:264] * SCALE).astype(BF)
    to_next[1] = vgacc[240:264].astype(BF)

    send_if(cp == 3, to_next.at[1], rel_next, hs.at[9], hr.at[9], across)
    send_if(cp == 4, to_prev.at[1], rel_prev, hs.at[9], hr.at[9], across)
    send_if(has_prev, to_prev.at[0], from_next.at[0], hs.at[6], hr.at[6], prv)
    send_if(has_next, to_next.at[0], from_prev.at[0], hs.at[7], hr.at[7], nxt)
    send_if(has_prev & (cp != 4), to_prev.at[1], from_next.at[1], hs.at[10], hr.at[10], prv)
    send_if(has_next & (cp != 3), to_next.at[1], from_prev.at[1], hs.at[11], hr.at[11], nxt)

    total = cpart[4 * core + x]
    landed(4, cxr.at[pl.ds(1, 7)])
    for k in range(1, 8):
        total = total + cxr[k]
    cz[z] = total
    spread(5, cz.at[pl.ds(0, 7)], [(cz.at[z], cz.at[z], z_peer(k)) for k in FAR])

    def inner_bwd(t, carry):
        backward_tile(1 + t)
        return carry

    lax.fori_loop(0, 2, inner_bwd, 0)
    outs.append(pltpu.make_async_copy(qg_v, qg_out.at[0], out_sem.at[2]))
    outs[-1].start()

    total = ys[y].astype(F32)
    landed(0, yr.at[pl.ds(1, 7)])
    for k in range(1, NY):
        total = total + yr[k].astype(F32)
    zr[z] = total.astype(BF)
    spread(2, zr.at[pl.ds(0, 7)], [(zr.at[z], zr.at[z], z_peer(k)) for k in FAR])
    total = bs[z].astype(F32)
    landed(1, br.at[pl.ds(1, 7)])
    for k in range(1, NZ):
        total = total + br[k].astype(F32)
    bsum[...] = total.astype(BF)
    bz[y] = bsum[yh]
    spread(3, bz.at[pl.ds(0, 7)], [(bsum.at[((y + k) % NY) // NYL], bz.at[y], y_peer(k)) for k in FAR])

    landed(5, cz.at[pl.ds(0, 7)])
    total = cz[0]
    for t in range(1, NZ):
        total = total + cz[t]
    cy[y] = total
    spread(6, cy.at[pl.ds(0, 7)], [(cy.at[y], cy.at[y], y_peer(k)) for k in FAR])

    landed(2, zr.at[pl.ds(0, 7)])
    total = zr[0].astype(F32)
    for t in range(1, NZ):
        total = total + zr[t].astype(F32)
    fin[4 * core + yl] = total.astype(BF)
    mine = fin.at[4 * core + yl]
    others = [(mine, mine, partner)]
    for k in (2, 1, 3):
        others += [(mine, mine, yl_peer(k)), (mine, mine, yl_peer(k, 1 - core))]
    spread(8, fin.at[pl.ds(0, 7)], others)
    landed(3, bz.at[pl.ds(0, 7)])
    total = bz[0].astype(F32)
    for t in range(1, NY):
        total = total + bz[t].astype(F32)
    finb[core, z] = total.astype(BF)
    mine = finb.at[core, z]
    spread(9, finb.at[core, pl.ds(0, 7)], [(mine, mine, z_peer(k)) for k in FAR])

    arrived_if(cp == 7, rel_next, hr.at[9], hs.at[9], across)
    send_if(cp == 7, rel_next, from_prev.at[1], hs.at[11], hr.at[11], cp_peer(5))
    arrived_if(cp == 0, rel_prev, hr.at[9], hs.at[9], across)
    send_if(cp == 0, rel_prev, from_next.at[1], hs.at[10], hr.at[10], cp_peer(3))

    landed(6, cy.at[pl.ds(0, 7)])
    total = cy[0]
    for t in range(1, NY):
        total = total + cy[t]
    cx[4 * core + x] = total
    mine = cx.at[4 * core + x]
    others = [(mine, mine, partner)]
    for k in range(1, NX):
        others += [(mine, mine, x_peer(k)), (mine, mine, x_peer(k, 1 - core))]
    spread(7, cx.at[pl.ds(0, 7)], others)

    landed(9, finb.at[core, pl.ds(0, 7)])
    spread(10, finb.at[core], [(finb.at[core], finb.at[core], partner)])

    arrived_if(has_next, from_next.at[0], hr.at[6], hs.at[6], prv)
    arrived_if(has_prev, from_prev.at[0], hr.at[7], hs.at[7], prv)
    arrived_if(has_next, from_next.at[1], hr.at[10], hs.at[10], prv)
    arrived_if(has_prev, from_prev.at[1], hr.at[11], hs.at[11], prv)
    for src, acc, dst, scale in ((0, kgacc, kg_v, SCALE), (1, vgacc, vg_v, 1.0)):
        low_rows = acc[48:80] * scale
        extra = from_prev[src].astype(F32)
        dst[0:32] = jnp.concatenate([low_rows[0:BLK] + extra, low_rows[BLK:32]], axis=0).astype(BF)
        dst[32:144] = (acc[80:192] * scale).astype(BF)
        dst[144:192] = (acc[192:240] * scale + from_next[src].astype(F32)).astype(BF)
    outs.append(pltpu.make_async_copy(kg_v, kg_out.at[0], out_sem.at[3]))
    outs[-1].start()
    outs.append(pltpu.make_async_copy(vg_v, vg_out.at[0], out_sem.at[4]))
    outs[-1].start()

    landed(7, cx.at[pl.ds(0, 7)])
    for h in range(2):
        for b in range(NX):
            at = h * HALF + b * 128
            cg_v[:, at:at + 128] = cx[4 * h + b, 0:KW]
    outs.append(pltpu.make_async_copy(cg_v, cg_out, out_sem.at[6]))
    outs[-1].start()

    landed(8, fin.at[pl.ds(0, 7)])
    for h in range(2):
        for t in range(NYL):
            wg_v[16 * t:16 * t + 16, h * HALF:h * HALF + CW] = fin[4 * h + t].astype(F32)
    landed(10, finb.at[1 - core])
    for h in range(2):
        for t in range(NZ):
            wg_v[8 * t:8 * t + 8, h * HALF + CW:h * HALF + HALF] = finb[h, t].astype(F32)
    outs.append(pltpu.make_async_copy(wg_v, wg_out, out_sem.at[5]))
    outs[-1].start()

    for c in sent:
        c.wait_send()
    for cond, c in sent_if:
        pl.when(cond)(c.wait_send)
    for c in outs:
        c.wait()


def finish(*refs):
    ins, outs, sem = refs[:6], refs[6:12], refs[12]
    copies = [pltpu.make_async_copy(a, b, sem.at[n]) for n, (a, b) in enumerate(zip(ins, outs))]
    for c in copies:
        c.start()
    for c in copies:
        c.wait()


def body(
    queries, key_rows, value_rows, stream_in, out_grad, out_weight, conv_weight, lengths, offsets
):
    hbm = pl.BlockSpec(memory_space=pltpu.HBM)
    free = pl.BlockSpec(memory_space=pl.ANY)
    dma = pltpu.SemaphoreType.DMA
    sds = jax.ShapeDtypeStruct
    V = pltpu.VMEM
    held = lambda a: pltpu.with_memory_space_constraint(a, pltpu.HBM)
    shapes = [
            sds((1, ROWS, HD), BF), sds((1, ROWS, HD), BF), sds((1, ROWS, HD), BF),
            sds((1, ROWS, D), BF), sds((64, D), F32), sds((KW, D), F32),
        ]
    made = pl.pallas_call(
        kernel,
        in_specs=[pl.BlockSpec(memory_space=pltpu.SMEM)] + [hbm] * 8,
        out_specs=[free] * 6,
        out_shape=shapes,
        scratch_shapes=[
            pltpu.SMEM((1, 2), jnp.int32), V((KW, D), F32),
            V((EXT, HD), BF), V((EXT, HD), BF), V((48, HD), BF), V((ROWS, HD), BF), V((ROWS, D), BF),
            V((GEXT, D), BF), V((8, GEXT, 128), F32), V((2, HD, HALF), BF),
            V((ROWS, HD), BF), V((ROWS, HD), BF), V((2, ROWS, HALF), BF), V((ROWS, HALF), BF),
            V((ROWS, HD), BF), V((4, 2, 4 * QT, KT), F32),
            V((EXT, HD), F32), V((EXT, HD), F32),
            V((2, 48, HD), BF), V((2, BLK, HD), BF), V((2, 48, HD), BF), V((2, BLK, HD), BF),
            V((48, HD), BF), V((BLK, HD), BF),
            V((ROWS, HD), BF), V((ROWS, HD), BF), V((ROWS, HD), BF), V((64, D), F32), V((KW, D), F32),
            V((NC, NX, 128, CW), BF), V((NC, 2, 128, CW), BF), V((NC, 2, 64, CW), BF), V((NC, 2, 64, CW), BF),
            V((NY, 16, CW), BF), V((NY, 16, CW), BF), V((NZ, 16, CW), BF), V((8, 16, CW), BF),
            V((NZ, 2, 8, CW), BF), V((NZ, 2, 8, CW), BF), V((2, 8, CW), BF), V((NY, 8, CW), BF),
            V((2, NZ, 8, CW), BF),
            V((8, 8, 128), F32), V((8, 8, 128), F32),
            V((NY, 8, 128), F32), V((NZ, 8, 128), F32), V((8, 8, 128), F32),
            dma((9,)), dma((7,)), dma((12,)), dma((12,)), dma((NC, 6)), dma((NC, 6)), dma((17,)), dma((17,)),
        ],
        compiler_params=pltpu.CompilerParams(
            collective_id=0, has_side_effects=True, vmem_limit_bytes=48 * 1024 * 1024
        ),
        name="fused_backward",
    )(lengths, *map(held, (
        offsets, queries, key_rows, value_rows, stream_in, out_grad, out_weight, conv_weight
    )))
    return pl.pallas_call(
        finish,
        in_specs=[free] * 6,
        out_specs=[free] * 6,
        out_shape=shapes,
        scratch_shapes=[dma((6,))],
        compiler_params=pltpu.CompilerParams(vmem_limit_bytes=1024 * 1024),
        name="finish",
    )(*made)


def solution(mesh):
    row = P("dp", "cp", None)
    return jax.shard_map(
        body,
        mesh=mesh,
        in_specs=(row, row, row, row, row, P("cp", None), P(), P("dp"), P("dp", None)),
        out_specs=(row, row, row, row, P("cp", None), P()),
        check_vma=False,
    )
```

```python
import jax
import jax.numpy as jnp
from jax import lax
from jax.experimental import pallas as pl
from jax.experimental.pallas import tpu as pltpu
from jax.sharding import PartitionSpec as P

HSZ = 64
BLK = 24
KW = 7
ROWS = 192
HD = 512
D = 1024
HALF = 512
NX, NY, NYL, NZ = 4, 8, 4, 8
NC = 2
CW = HALF // NC
QT = 48
KT = 128
EXT = 272
GEXT = 208
NEG = -1e30
SCALE = HSZ ** -0.5
BF = jnp.bfloat16
F32 = jnp.float32
MESH = pl.DeviceIdType.MESH
FAR = (4, 3, 5, 2, 6, 1, 7)

CONTRACT_LAST = (((1,), (1,)), ((), ()))
CONTRACT_FIRST = (((0,), (0,)), ((), ()))
PLAIN = (((1,), (0,)), ((), ()))


def dot(a, b, dims):
    return lax.dot_general(a, b, dims, preferred_element_type=F32)


def kernel(
    len_ref, off_in, q_in, k_in, v_in, s_in, g_in, w_in, cw_in,
    qg_out, kg_out, vg_out, sg_out, wg_out, cg_out,
    off_ref, cw_ref, kext, vext, vrel, qbuf, sbuf, gext, gf, wh, a_own, a_par, sg, s2p, ag, psave,
    kgacc, vgacc, to_prev, to_next, from_next, from_prev, rel_prev, rel_next,
    qg_v, kg_v, vg_v, wg_v, cg_v,
    xs, xr, xc, xrel, ys, yr, zr, fin, bs, br, bsum, bz, finb,
    cpart, cxr, cy, cz, cx,
    loc, out_sem, hs, hr, xss, xrs, gs, gr,
):
    cp = lax.axis_index("cp")
    dp = lax.axis_index("dp")
    yh = cp // NX
    x = cp % NX
    core = dp % 2
    z = (dp // 2) % NZ
    yl = dp // (2 * NZ)
    y = yh * NYL + yl

    def dev(y_to, x_to, z_to, core_to):
        return {
            "cp": (y_to // NYL) * NX + x_to,
            "dp": ((y_to % NYL) * NZ + z_to) * 2 + core_to,
        }

    def x_peer(k, to_core=None):
        return dev(y, (x + k) % NX, z, core if to_core is None else to_core)

    def y_peer(k):
        return dev((y + k) % NY, x, z, core)

    def z_peer(k):
        return dev(y, x, (z + k) % NZ, core)

    def yl_peer(k, to_core=None):
        return dev(yh * NYL + (yl + k) % NYL, x, z, core if to_core is None else to_core)

    partner = dev(y, x, z, 1 - core)

    def cp_peer(k):
        return {"cp": (cp + k) % 8, "dp": dp}

    nxt, prv, across = cp_peer(1), cp_peer(7), cp_peer(4)

    def rc(src, dst, ssem, rsem, to):
        return pltpu.make_async_remote_copy(
            src_ref=src, dst_ref=dst, send_sem=ssem, recv_sem=rsem,
            device_id=to, device_id_type=MESH,
        )

    sent = []
    sent_if = []

    def send(src, dst, ssem, rsem, to):
        c = rc(src, dst, ssem, rsem, to)
        c.start()
        sent.append(c)

    def send_if(cond, src, dst, ssem, rsem, to):
        c = rc(src, dst, ssem, rsem, to)
        pl.when(cond)(c.start)
        sent_if.append((cond, c))

    def spread(n, whole, copies):
        for src, dst, to in copies:
            rc(src, dst, gs.at[n], gr.at[n], to).start()
        sent.append(rc(whole, whole, gs.at[n], gr.at[n], partner))

    def landed(n, whole):
        rc(whole, whole, gs.at[n], gr.at[n], partner).wait_recv()

    def arrived(dst, rsem, ssem, to):
        rc(dst, dst, ssem, rsem, to).wait_recv()

    def arrived_if(cond, dst, rsem, ssem, to):
        pl.when(cond)(rc(dst, dst, ssem, rsem, to).wait_recv)

    barrier = pltpu.get_barrier_semaphore()
    greet = [y_peer(k) for k in (4, 3, 5, 2, 6, 1, 7)]
    greet += [z_peer(k) for k in (4, 3, 5, 2, 6, 1, 7)]
    greet += [nxt, prv] + [x_peer(k) for k in (2, 1, 3)] + [partner]
    greet += [yl_peer(k, 1 - core) for k in (2, 1, 3)] + [x_peer(k, 1 - core) for k in (2, 1, 3)] + [cp_peer(3), cp_peer(5)]
    for to in greet:
        pl.semaphore_signal(barrier, inc=1, device_id=to, device_id_type=MESH)

    c512 = pl.multiple_of(core * HALF, HALF)
    cprow = pl.multiple_of(cp * 64, 64)
    orow = pl.multiple_of(((cp + 4) % 8) * 64, 64)
    ylrow = pl.multiple_of(yl * 16, 16)
    wq_mine = pl.multiple_of(cp * 64 + yl * 16, 16)

    loads = [
        pltpu.make_async_copy(k_in.at[0], kext.at[pl.ds(48, ROWS)], loc.at[0]),
        pltpu.make_async_copy(q_in.at[0], qbuf, loc.at[1]),
        pltpu.make_async_copy(v_in.at[0], vext.at[pl.ds(48, ROWS)], loc.at[2]),
        pltpu.make_async_copy(g_in.at[0], gext.at[pl.ds(8, ROWS)], loc.at[3]),
        pltpu.make_async_copy(w_in.at[:, pl.ds(0, HALF)], wh.at[0, pl.ds(cprow, 64)], loc.at[4]),
        pltpu.make_async_copy(w_in.at[:, pl.ds(HALF, HALF)], wh.at[1, pl.ds(cprow, 64)], loc.at[5]),
        pltpu.make_async_copy(s_in.at[0], sbuf, loc.at[6]),
        pltpu.make_async_copy(off_in, off_ref, loc.at[7]),
        pltpu.make_async_copy(cw_in, cw_ref, loc.at[8]),
    ]
    for n in (7, 0, 1, 2, 3, 8, 4, 5, 6):
        loads[n].start()

    has_prev = cp > 0
    has_next = cp < 7
    kext[264:272] = jnp.zeros((8, HD), BF)
    vext[264:272] = jnp.zeros((8, HD), BF)
    to_clear = jnp.zeros((48, HD), BF)

    @pl.when(cp == 0)
    def _():
        kext[0:48] = to_clear
        vext[0:48] = to_clear
        gext[0:8] = jnp.zeros((8, D), BF)
        from_prev[...] = jnp.zeros((2, BLK, HD), BF)

    @pl.when(cp == 7)
    def _():
        kext[240:264] = to_clear[0:BLK]
        vext[240:264] = to_clear[0:BLK]
        gext[200:208] = jnp.zeros((8, D), BF)
        from_next[...] = jnp.zeros((2, 48, HD), BF)

    loads[7].wait()
    length = len_ref[0]
    back = off_ref[0, 0]
    ahead = off_ref[0, 1]
    lane = lax.broadcasted_iota(jnp.int32, (1, 256), 1)
    head_f = [((lane // HSZ) == h).astype(F32) for h in range(4)]
    head_b = [m.astype(BF) for m in head_f]
    row_i = lax.broadcasted_iota(jnp.int32, (4 * QT, KT), 0)
    col_i = lax.broadcasted_iota(jnp.int32, (4 * QT, KT), 1)
    rel = col_i // BLK - 2 - (row_i % QT) // BLK
    reach = (rel >= -back) & (rel <= ahead)

    def stacked(block):
        return jnp.concatenate([block * head_b[h] for h in range(4)], axis=0)

    def unstacked(block):
        total = block[0:QT] * head_f[0]
        for h in range(1, 4):
            total = total + block[h * QT:(h + 1) * QT] * head_f[h]
        return total

    def forward_tile(i):
        r0 = pl.multiple_of(i * QT, 16)
        key_frame = cp * ROWS + i * QT - 2 * BLK + col_i
        ok = reach & (key_frame >= 0) & (key_frame < length)
        frame = cp * ROWS + i * QT + lax.broadcasted_iota(jnp.int32, (QT, 1), 0)
        valid = (frame < length).astype(F32)
        for g in range(2):
            cols = slice(256 * g, 256 * g + 256)
            kk = kext[pl.ds(r0, KT), cols]
            vv = vext[pl.ds(r0, KT), cols]
            qs = stacked(qbuf[pl.ds(r0, QT), cols])
            s = jnp.where(ok, dot(qs, kk, CONTRACT_LAST) * SCALE, NEG)
            e = jnp.exp(s - jnp.max(s, axis=1, keepdims=True))
            p = e / jnp.sum(e, axis=1, keepdims=True)
            psave[i, g] = p
            o = unstacked(dot(p.astype(BF), vv, PLAIN))
            a_own[pl.ds(r0, QT), cols] = (o * valid).astype(BF)

    for n in (0, 1, 2):
        loads[n].wait()

    def inner_fwd(t, carry):
        forward_tile(1 + t)
        return carry

    lax.fori_loop(0, 2, inner_fwd, 0)

    pl.semaphore_wait(barrier, len(greet))

    gi, ki, vi = g_in.at[0], k_in.at[0], v_in.at[0]
    k_lo, k_hi = kext.at[pl.ds(0, 48)], kext.at[pl.ds(240, BLK)]
    v_lo, v_hi = vext.at[pl.ds(0, 48)], vext.at[pl.ds(240, BLK)]
    g_lo, g_hi = gext.at[pl.ds(0, 8)], gext.at[pl.ds(200, 8)]
    send_if(has_next, gi.at[pl.ds(184, 8)], g_lo, hs.at[0], hr.at[0], nxt)
    send_if(has_prev, gi.at[pl.ds(0, 8)], g_hi, hs.at[1], hr.at[1], prv)
    wq = wh.at[core, pl.ds(wq_mine, 16)]
    o_block = wh.at[core, pl.ds(orow, 64)]
    three = wh.at[core, pl.ds(0, 192)]
    spread(12, o_block, [
        (w_in.at[pl.ds(ylrow, 16), pl.ds(c512, HALF)], wq, dev((1 - yh) * NYL + k, x, z, core))
        for k in range(NYL)
    ])
    v_last, v_first = vi.at[pl.ds(144, 48)], vi.at[pl.ds(0, BLK)]
    send_if(cp == 3, v_last, vrel, hs.at[8], hr.at[8], across)
    send_if(cp == 4, v_first, vrel.at[pl.ds(0, BLK)], hs.at[8], hr.at[8], across)
    send_if(has_next, ki.at[pl.ds(144, 48)], k_lo, hs.at[2], hr.at[2], nxt)
    send_if(has_prev, ki.at[pl.ds(0, BLK)], k_hi, hs.at[3], hr.at[3], prv)
    send_if(has_next & (cp != 3), v_last, v_lo, hs.at[4], hr.at[4], nxt)
    send_if(has_prev & (cp != 4), v_first, v_hi, hs.at[5], hr.at[5], prv)
    spread(11, three, [
        (w_in.at[:, pl.ds(c512, HALF)], wh.at[core, pl.ds(cprow, 64)], x_peer(k)) for k in range(1, NX)
    ])

    loads[3].wait()
    loads[8].wait()

    def tap_sum(n, lanes, r0, r1):
        acc = jnp.zeros((r1 - r0, 128), F32)
        for j in range(KW):
            acc = acc + cw_ref[pl.ds(j, 1), lanes] * gf[n, pl.ds(r0 + 11 - j, r1 - r0), :]
        frame = cp * ROWS + r0 + lax.broadcasted_iota(jnp.int32, (r1 - r0, 128), 0)
        at = pl.ds(pl.multiple_of((n % 4) * 128, 128), 128)
        sg[n // 4, r0:r1, at] = jnp.where(frame < length, acc, 0.0).astype(BF)

    def masked_rows(n, lanes, r0, r1):
        frame = cp * ROWS - 8 + r0 + lax.broadcasted_iota(jnp.int32, (r1 - r0, 128), 0)
        ok = (frame >= 0) & (frame < length)
        gf[n, r0:r1] = jnp.where(ok, gext[r0:r1, lanes].astype(F32), 0.0)

    def conv_inside(n, carry):
        lanes = pl.ds(pl.multiple_of(n * 128, 128), 128)
        masked_rows(n, lanes, 8, 200)
        tap_sum(n, lanes, 16, 176)
        return carry

    def conv_edges(n, carry):
        lanes = pl.ds(pl.multiple_of(n * 128, 128), 128)
        masked_rows(n, lanes, 0, 8)
        masked_rows(n, lanes, 200, 208)
        tap_sum(n, lanes, 0, 16)
        tap_sum(n, lanes, 176, 192)
        return carry

    lax.fori_loop(0, 8, conv_inside, 0)

    arrived_if(has_prev, g_lo, hr.at[0], hs.at[0], nxt)
    arrived_if(has_next, g_hi, hr.at[1], hs.at[1], nxt)

    lax.fori_loop(0, 8, conv_edges, 0)
    send(sg.at[1 - core], s2p, gs.at[15], gr.at[15], partner)
    outs = [
        pltpu.make_async_copy(sg.at[0], sg_out.at[0, :, pl.ds(0, HALF)], out_sem.at[0]),
        pltpu.make_async_copy(sg.at[1], sg_out.at[0, :, pl.ds(HALF, HALF)], out_sem.at[1]),
    ]
    outs[0].start()
    outs[1].start()

    arrived_if(cp == 7, vrel, hr.at[8], hs.at[8], across)
    send_if(cp == 7, vrel, v_lo, hs.at[4], hr.at[4], cp_peer(5))
    arrived_if(cp == 0, vrel.at[pl.ds(0, BLK)], hr.at[8], hs.at[8], across)
    send_if(cp == 0, vrel.at[pl.ds(0, BLK)], v_hi, hs.at[5], hr.at[5], cp_peer(3))
    landed(12, o_block)
    spread(13, three, [(o_block, o_block, x_peer(k)) for k in range(1, NX)])

    landed(11, three)

    def whole_block(side, k):
        return wh.at[core, pl.ds(pl.multiple_of((side * NX + (x + NX - k) % NX) * 64, 64), 64)]

    near = [o_block] + [whole_block(yh, k) for k in range(1, NX)]
    for block in near:
        rc(block, block, gs.at[14], gr.at[14], partner).start()

    arrived_if(has_prev, k_lo, hr.at[2], hs.at[2], nxt)
    arrived_if(has_next, k_hi, hr.at[3], hs.at[3], nxt)
    arrived_if(has_prev, v_lo, hr.at[4], hs.at[4], nxt)
    arrived_if(has_next, v_hi, hr.at[5], hs.at[5], nxt)

    def edge_fwd(t, carry):
        forward_tile(3 * t)
        return carry

    lax.fori_loop(0, 2, edge_fwd, 0)
    send(a_own, a_par, gs.at[16], gr.at[16], partner)

    arrived(s2p, gr.at[15], gs.at[15], partner)
    arrived(a_par, gr.at[16], gs.at[16], partner)

    low, high = pl.ds(0, 64), pl.ds(64, 64)
    far = (x + 2) % NX
    for w in range(2):
        cs = slice(w * 256, w * 256 + 256)
        dw = dot(a_own[...], sg[core, :, cs], CONTRACT_FIRST)
        dw = dw + dot(a_par[...], s2p[:, cs], CONTRACT_FIRST)
        dw = dw.astype(BF)
        per = 256 // CW
        for u in range(per):
            c = w * per + u
            us = slice(u * CW, u * CW + CW)
            for xt in range(NX):
                xs[c, xt, 0:64] = dw[64 * xt:64 * xt + 64, us]
                xs[c, xt, 64:128] = dw[256 + 64 * xt:256 + 64 * xt + 64, us]
            send(xs.at[c, far, low], xrel.at[c, 0], xss.at[c, 0], xrs.at[c, 0], x_peer(1))
            send(xs.at[c, far, high], xrel.at[c, 1], xss.at[c, 1], xrs.at[c, 1], x_peer(3))
        for u in range(per):
            c = w * per + u
            send(xs.at[c, (x + 1) % NX, high], xr.at[c, 0, high], xss.at[c, 2], xrs.at[c, 2], x_peer(1))
            send(xs.at[c, (x + 3) % NX, low], xr.at[c, 1, low], xss.at[c, 3], xrs.at[c, 3], x_peer(3))

    landed(13, three)
    spread(14, wh.at[core, pl.ds(0, 448)], [
        (whole_block(1 - yh, k), whole_block(1 - yh, k), partner) for k in range(1, NX)
    ])

    for c in range(NC):
        arrived(xrel.at[c, 0], xrs.at[c, 0], xss.at[c, 0], partner)
        xc[c, 0] = (xs[c, (x + 1) % NX, 0:64].astype(F32) + xrel[c, 0].astype(F32)).astype(BF)
        send(xc.at[c, 0], xr.at[c, 0, low], xss.at[c, 4], xrs.at[c, 4], x_peer(1))
        arrived(xrel.at[c, 1], xrs.at[c, 1], xss.at[c, 1], partner)
        xc[c, 1] = (xs[c, (x + 3) % NX, 64:128].astype(F32) + xrel[c, 1].astype(F32)).astype(BF)
        send(xc.at[c, 1], xr.at[c, 1, high], xss.at[c, 5], xrs.at[c, 5], x_peer(3))

    def x_sum(c):
        arrived(xr.at[c, 0, high], xrs.at[c, 2], xss.at[c, 2], partner)
        arrived(xr.at[c, 1, low], xrs.at[c, 3], xss.at[c, 3], partner)
        arrived(xr.at[c, 0, low], xrs.at[c, 4], xss.at[c, 4], partner)
        arrived(xr.at[c, 1, high], xrs.at[c, 5], xss.at[c, 5], partner)
        total = xs[c, x].astype(F32) + xr[c, 0].astype(F32) + xr[c, 1].astype(F32)
        return total

    ys[...] = x_sum(0).astype(BF).reshape(NY, 16, CW)
    spread(0, ys.at[pl.ds(0, 7)], [(ys.at[(y + k) % NY], yr.at[k], y_peer(k)) for k in FAR])
    total = x_sum(1)
    for t in range(NZ):
        for h in range(2):
            bs[t, h] = total[64 * h + 8 * t:64 * h + 8 * t + 8].astype(BF)
    spread(1, bs.at[pl.ds(0, 7)], [(bs.at[(z + k) % NZ], br.at[k], z_peer(k)) for k in FAR])

    loads[4].wait()
    loads[5].wait()
    loads[6].wait()
    landed(14, wh.at[1 - core, pl.ds(0, 448)])

    t_frame = cp * ROWS + lax.broadcasted_iota(jnp.int32, (ROWS, 128), 0)
    t_valid = (t_frame < length).astype(F32)

    def tap_chunk(m, carry):
        at = pl.ds(pl.multiple_of((m % 2) * 256, 256), 256)
        proj = dot(a_own[...], wh[m // 2, :, at], PLAIN)
        for u in range(2):
            n = 2 * m + u
            lanes = pl.ds(pl.multiple_of(n * 128, 128), 128)
            mixed = (sbuf[:, lanes].astype(F32) + proj[:, 128 * u:128 * u + 128]) * t_valid
            rows = [
                jnp.sum(mixed * gf[n, pl.ds(11 - j, ROWS), :], axis=0, keepdims=True)
                for j in range(KW)
            ]
            rows.append(jnp.zeros((1, 128), F32))
            cpart[n] = jnp.concatenate(rows, axis=0)
        return carry

    lax.fori_loop(0, 4, tap_chunk, 0)
    taps = [(cpart.at[4 * (1 - core) + x], cxr.at[4], partner)]
    for k in range(1, NX):
        to_x = (x + k) % NX
        taps.append((cpart.at[4 * core + to_x], cxr.at[k], x_peer(k)))
        taps.append((cpart.at[4 * (1 - core) + to_x], cxr.at[4 + k], x_peer(k, 1 - core)))
    spread(4, cpart.at[pl.ds(0, 7)], taps)

    grad_att = dot(sg[0], wh[0], CONTRACT_LAST) + dot(sg[1], wh[1], CONTRACT_LAST)
    ag[...] = grad_att.astype(BF)
    kgacc[...] = jnp.zeros((EXT, HD), F32)
    vgacc[...] = jnp.zeros((EXT, HD), F32)

    def backward_tile(i):
        r0 = pl.multiple_of(i * QT, 16)
        for g in range(2):
            cols = slice(256 * g, 256 * g + 256)
            kk = kext[pl.ds(r0, KT), cols]
            vv = vext[pl.ds(r0, KT), cols]
            qs = stacked(qbuf[pl.ds(r0, QT), cols])
            gs = stacked(ag[pl.ds(r0, QT), cols])
            p = psave[i, g]
            dprob = dot(gs, vv, CONTRACT_LAST)
            inner = jnp.sum(p * dprob, axis=1, keepdims=True)
            ds = (p * (dprob - inner)).astype(BF)
            qg_v[pl.ds(r0, QT), cols] = (unstacked(dot(ds, kk, PLAIN)) * SCALE).astype(BF)
            at = pl.ds(r0, KT)
            kgacc[at, cols] = kgacc[at, cols] + dot(ds, qs, CONTRACT_FIRST)
            vgacc[at, cols] = vgacc[at, cols] + dot(p.astype(BF), gs, CONTRACT_FIRST)

    def edge_bwd(t, carry):
        backward_tile(3 * t)
        return carry

    lax.fori_loop(0, 2, edge_bwd, 0)
    to_prev[0] = (kgacc[0:48] * SCALE).astype(BF)
    to_prev[1] = vgacc[0:48].astype(BF)
    to_next[0] = (kgacc[240:264] * SCALE).astype(BF)
    to_next[1] = vgacc[240:264].astype(BF)

    send_if(cp == 3, to_next.at[1], rel_next, hs.at[9], hr.at[9], across)
    send_if(cp == 4, to_prev.at[1], rel_prev, hs.at[9], hr.at[9], across)
    send_if(has_prev, to_prev.at[0], from_next.at[0], hs.at[6], hr.at[6], prv)
    send_if(has_next, to_next.at[0], from_prev.at[0], hs.at[7], hr.at[7], nxt)
    send_if(has_prev & (cp != 4), to_prev.at[1], from_next.at[1], hs.at[10], hr.at[10], prv)
    send_if(has_next & (cp != 3), to_next.at[1], from_prev.at[1], hs.at[11], hr.at[11], nxt)

    total = cpart[4 * core + x]
    landed(4, cxr.at[pl.ds(1, 7)])
    for k in range(1, 8):
        total = total + cxr[k]
    cz[z] = total
    spread(5, cz.at[pl.ds(0, 7)], [(cz.at[z], cz.at[z], z_peer(k)) for k in FAR])

    def inner_bwd(t, carry):
        backward_tile(1 + t)
        return carry

    lax.fori_loop(0, 2, inner_bwd, 0)
    outs.append(pltpu.make_async_copy(qg_v, qg_out.at[0], out_sem.at[2]))
    outs[-1].start()

    total = ys[y].astype(F32)
    landed(0, yr.at[pl.ds(1, 7)])
    for k in range(1, NY):
        total = total + yr[k].astype(F32)
    zr[z] = total.astype(BF)
    spread(2, zr.at[pl.ds(0, 7)], [(zr.at[z], zr.at[z], z_peer(k)) for k in FAR])
    total = bs[z].astype(F32)
    landed(1, br.at[pl.ds(1, 7)])
    for k in range(1, NZ):
        total = total + br[k].astype(F32)
    bsum[...] = total.astype(BF)
    bz[y] = bsum[yh]
    spread(3, bz.at[pl.ds(0, 7)], [(bsum.at[((y + k) % NY) // NYL], bz.at[y], y_peer(k)) for k in FAR])

    landed(5, cz.at[pl.ds(0, 7)])
    total = cz[0]
    for t in range(1, NZ):
        total = total + cz[t]
    cy[y] = total
    spread(6, cy.at[pl.ds(0, 7)], [(cy.at[y], cy.at[y], y_peer(k)) for k in FAR])

    landed(2, zr.at[pl.ds(0, 7)])
    total = zr[0].astype(F32)
    for t in range(1, NZ):
        total = total + zr[t].astype(F32)
    fin[4 * core + yl] = total.astype(BF)
    mine = fin.at[4 * core + yl]
    others = [(mine, mine, partner)]
    for k in (2, 1, 3):
        others += [(mine, mine, yl_peer(k)), (mine, mine, yl_peer(k, 1 - core))]
    spread(8, fin.at[pl.ds(0, 7)], others)
    landed(3, bz.at[pl.ds(0, 7)])
    total = bz[0].astype(F32)
    for t in range(1, NY):
        total = total + bz[t].astype(F32)
    finb[core, z] = total.astype(BF)
    mine = finb.at[core, z]
    spread(9, finb.at[core, pl.ds(0, 7)], [(mine, mine, z_peer(k)) for k in FAR])

    arrived_if(cp == 7, rel_next, hr.at[9], hs.at[9], across)
    send_if(cp == 7, rel_next, from_prev.at[1], hs.at[11], hr.at[11], cp_peer(5))
    arrived_if(cp == 0, rel_prev, hr.at[9], hs.at[9], across)
    send_if(cp == 0, rel_prev, from_next.at[1], hs.at[10], hr.at[10], cp_peer(3))

    landed(6, cy.at[pl.ds(0, 7)])
    total = cy[0]
    for t in range(1, NY):
        total = total + cy[t]
    cx[4 * core + x] = total
    mine = cx.at[4 * core + x]
    others = [(mine, mine, partner)]
    for k in range(1, NX):
        others += [(mine, mine, x_peer(k)), (mine, mine, x_peer(k, 1 - core))]
    spread(7, cx.at[pl.ds(0, 7)], others)

    landed(9, finb.at[core, pl.ds(0, 7)])
    spread(10, finb.at[core], [(finb.at[core], finb.at[core], partner)])

    arrived_if(has_next, from_next.at[0], hr.at[6], hs.at[6], prv)
    arrived_if(has_prev, from_prev.at[0], hr.at[7], hs.at[7], prv)
    arrived_if(has_next, from_next.at[1], hr.at[10], hs.at[10], prv)
    arrived_if(has_prev, from_prev.at[1], hr.at[11], hs.at[11], prv)
    for src, acc, dst, scale in ((0, kgacc, kg_v, SCALE), (1, vgacc, vg_v, 1.0)):
        low_rows = acc[48:80] * scale
        extra = from_prev[src].astype(F32)
        dst[0:32] = jnp.concatenate([low_rows[0:BLK] + extra, low_rows[BLK:32]], axis=0).astype(BF)
        dst[32:144] = (acc[80:192] * scale).astype(BF)
        dst[144:192] = (acc[192:240] * scale + from_next[src].astype(F32)).astype(BF)
    outs.append(pltpu.make_async_copy(kg_v, kg_out.at[0], out_sem.at[3]))
    outs[-1].start()
    outs.append(pltpu.make_async_copy(vg_v, vg_out.at[0], out_sem.at[4]))
    outs[-1].start()

    landed(7, cx.at[pl.ds(0, 7)])
    for h in range(2):
        for b in range(NX):
            at = h * HALF + b * 128
            cg_v[:, at:at + 128] = cx[4 * h + b, 0:KW]
    outs.append(pltpu.make_async_copy(cg_v, cg_out, out_sem.at[6]))
    outs[-1].start()

    landed(8, fin.at[pl.ds(0, 7)])
    for h in range(2):
        for t in range(NYL):
            wg_v[16 * t:16 * t + 16, h * HALF:h * HALF + CW] = fin[4 * h + t].astype(F32)
    landed(10, finb.at[1 - core])
    for h in range(2):
        for t in range(NZ):
            wg_v[8 * t:8 * t + 8, h * HALF + CW:h * HALF + HALF] = finb[h, t].astype(F32)
    outs.append(pltpu.make_async_copy(wg_v, wg_out, out_sem.at[5]))
    outs[-1].start()

    for c in sent:
        c.wait_send()
    for cond, c in sent_if:
        pl.when(cond)(c.wait_send)
    for c in outs:
        c.wait()


def finish(*refs):
    ins, outs, sem = refs[:6], refs[6:12], refs[12]
    copies = [pltpu.make_async_copy(a, b, sem.at[n]) for n, (a, b) in enumerate(zip(ins, outs))]
    for c in copies:
        c.start()
    for c in copies:
        c.wait()


def body(
    queries, key_rows, value_rows, stream_in, out_grad, out_weight, conv_weight, lengths, offsets
):
    hbm = pl.BlockSpec(memory_space=pltpu.HBM)
    free = pl.BlockSpec(memory_space=pl.ANY)
    dma = pltpu.SemaphoreType.DMA
    sds = jax.ShapeDtypeStruct
    V = pltpu.VMEM
    held = lambda a: pltpu.with_memory_space_constraint(a, pltpu.HBM)
    shapes = [
            sds((1, ROWS, HD), BF), sds((1, ROWS, HD), BF), sds((1, ROWS, HD), BF),
            sds((1, ROWS, D), BF), sds((64, D), F32), sds((KW, D), F32),
        ]
    made = pl.pallas_call(
        kernel,
        in_specs=[pl.BlockSpec(memory_space=pltpu.SMEM)] + [hbm] * 8,
        out_specs=[free] * 6,
        out_shape=shapes,
        scratch_shapes=[
            pltpu.SMEM((1, 2), jnp.int32), V((KW, D), F32),
            V((EXT, HD), BF), V((EXT, HD), BF), V((48, HD), BF), V((ROWS, HD), BF), V((ROWS, D), BF),
            V((GEXT, D), BF), V((8, GEXT, 128), F32), V((2, HD, HALF), BF),
            V((ROWS, HD), BF), V((ROWS, HD), BF), V((2, ROWS, HALF), BF), V((ROWS, HALF), BF),
            V((ROWS, HD), BF), V((4, 2, 4 * QT, KT), F32),
            V((EXT, HD), F32), V((EXT, HD), F32),
            V((2, 48, HD), BF), V((2, BLK, HD), BF), V((2, 48, HD), BF), V((2, BLK, HD), BF),
            V((48, HD), BF), V((BLK, HD), BF),
            V((ROWS, HD), BF), V((ROWS, HD), BF), V((ROWS, HD), BF), V((64, D), F32), V((KW, D), F32),
            V((NC, NX, 128, CW), BF), V((NC, 2, 128, CW), BF), V((NC, 2, 64, CW), BF), V((NC, 2, 64, CW), BF),
            V((NY, 16, CW), BF), V((NY, 16, CW), BF), V((NZ, 16, CW), BF), V((8, 16, CW), BF),
            V((NZ, 2, 8, CW), BF), V((NZ, 2, 8, CW), BF), V((2, 8, CW), BF), V((NY, 8, CW), BF),
            V((2, NZ, 8, CW), BF),
            V((8, 8, 128), F32), V((8, 8, 128), F32),
            V((NY, 8, 128), F32), V((NZ, 8, 128), F32), V((8, 8, 128), F32),
            dma((9,)), dma((7,)), dma((12,)), dma((12,)), dma((NC, 6)), dma((NC, 6)), dma((17,)), dma((17,)),
        ],
        compiler_params=pltpu.CompilerParams(
            collective_id=0, has_side_effects=True, vmem_limit_bytes=48 * 1024 * 1024
        ),
        name="fused_backward",
    )(lengths, *map(held, (
        offsets, queries, key_rows, value_rows, stream_in, out_grad, out_weight, conv_weight
    )))
    return pl.pallas_call(
        finish,
        in_specs=[free] * 6,
        out_specs=[free] * 6,
        out_shape=shapes,
        scratch_shapes=[dma((6,))],
        compiler_params=pltpu.CompilerParams(vmem_limit_bytes=1024 * 1024),
        name="finish",
    )(*made)


def solution(mesh):
    row = P("dp", "cp", None)
    return jax.shard_map(
        body,
        mesh=mesh,
        in_specs=(row, row, row, row, row, P("cp", None), P(), P("dp"), P("dp", None)),
        out_specs=(row, row, row, row, P("cp", None), P()),
        check_vma=False,
    )
```
